256 devices in a mesh: member: 8 (over z_lo, core), section: 4 (over x), atoms: 8 (over y, z_hi).
Axes of the slice: x: 4, y: 4, z: 8 (z_hi: 2, z_lo: 4; z = z_hi * 4 + z_lo), core: 2. Of those that a mesh axis runs over, the one named last changes fastest.
Arguments:
- positions: float32 [8, 3, 1024], P(None, None, 'atoms'), may hold values from -8 to 8
- atom_types: int32 [8, 1024], P(None, 'atoms'), may hold values from 0 to 127
- neighbors: int32 [8, 1024, 128], P(None, 'atoms'), may hold values from 0 to 1023
- nbr_mask: int32 [8, 1024, 128], P(None, 'atoms'), may hold values 0 or 1
- type_table: bfloat16 [8, 128, 128], P('member'), may hold values from -6 to 6
- norm_gain: bfloat16 [8, 4, 128], P('member', 'section'), may hold values from 0.25 to 1.75
- proj_weight: bfloat16 [8, 4, 128, 384], P('member', 'section'), may hold values from -0.5 to 0.5
- out_weight: bfloat16 [8, 4, 128, 128], P('member', 'section'), may hold values from -0.5 to 0.5
- force_coef: bfloat16 [8, 4, 4], P('member', 'section'), may hold values from -48 to 48
Outputs:
- atom_dev: float32 [8, 1024], P('section', 'atoms')
- max_dev: float32 [8], P('section')
- mean_force: float32 [8, 3, 1024], P('section', None, 'atoms')
The draws below stay inside these ranges and needn't reach their ends.
Inputs may be any that keep to these rules, and one draw needn't show every extreme that they name: `neighbors`: indices of atoms of the same frame, repeats and the atom itself allowed.
All inputs are finite; a program needn't handle non-finite values. No bound on the sum of `nbr_mask` on one device may be relied on, other than what follows from the above.
Results may differ from the reference program's by a relative error of at most 0.013.
Values may be sent and summed in bfloat16 or wider, within the bound.
A program may use at most 64 MiB of HBM per device.

```python
import math
import jax
import jax.numpy as jnp
from jax import lax

D = 128
HEADS = 4
NBR = 128
NTYPES = 128
MICRO = 8
HEAD_DIM = 32
ATOMS = 1024
MEMBERS = 8
SECTIONS = 4


def with_ends(array, stream_key, least, largest):
    index_at = [jax.random.randint(jax.random.fold_in(stream_key, axis), (), 0, length) for axis, length in enumerate(array.shape)]
    widest = array.shape.index(max(array.shape))
    next_to = index_at[:widest] + [(index_at[widest] + 1) % array.shape[widest]] + index_at[widest + 1:]
    return array.at[tuple(index_at)].set(least).at[tuple(next_to)].set(largest)


def block_scale(own_key, shape, pieces, smallest, top_value):
    def one(position, parts):
        draws = jax.random.uniform(jax.random.fold_in(jax.random.fold_in(own_key, 6), position), (parts,), jnp.float32, smallest / len(pieces), top_value / len(pieces))
        return jnp.repeat(jnp.exp(draws), shape[position] // parts).reshape((-1,) + (1,) * (len(shape) - position - 1))

    loudness = one(*pieces[0])
    for cut in pieces[1:]:
        loudness = loudness * one(*cut)
    return loudness


def gaussian(stream_key, extent, deviation, bound, cuts=(), kind=jnp.bfloat16):
    level = block_scale(stream_key, extent, cuts, -0.22, 0.18) if cuts else 1.0
    result = jax.random.normal(stream_key, extent, jnp.float32) * deviation * level
    return jnp.minimum(jnp.maximum(result, -bound), bound).astype(kind)


def setup_inputs(seed: int = 0) -> dict:
    streams_of = jax.random.split(jax.random.key(seed), 10)
    return {
        "positions": gaussian(streams_of[0], (MICRO, 3, ATOMS), 2.0, 8.0, ((2, 8),), jnp.float32),
        "atom_types": with_ends(jax.random.randint(streams_of[1], (MICRO, ATOMS), 0, NTYPES), jax.random.fold_in(streams_of[1], 1), 0, NTYPES - 1).astype(jnp.int32),
        "neighbors": with_ends(jax.random.randint(streams_of[2], (MICRO, ATOMS, NBR), 0, ATOMS), jax.random.fold_in(streams_of[2], 1), 0, ATOMS - 1).astype(jnp.int32),
        "nbr_mask": with_ends((jax.random.randint(streams_of[3], (MICRO, ATOMS, NBR), 0, 4) < 3).astype(jnp.int32), jax.random.fold_in(streams_of[3], 1), 0, 1),
        "type_table": gaussian(streams_of[4], (MEMBERS, NTYPES, D), 1.0, 6.0, ((0, 8),)),
        "norm_gain": jnp.clip(1.0 + 0.15 * jax.random.normal(streams_of[5], (MEMBERS, SECTIONS, D), jnp.float32), 0.25, 1.75).astype(jnp.bfloat16),
        "proj_weight": gaussian(streams_of[6], (MEMBERS, SECTIONS, D, 3 * D), D ** -0.5, 0.5, ((0, 8), (1, 4))),
        "out_weight": gaussian(streams_of[7], (MEMBERS, SECTIONS, D, D), D ** -0.5, 0.5, ((0, 8), (1, 4))),
        "force_coef": gaussian(streams_of[8], (MEMBERS, SECTIONS, HEADS), 16.0, 48.0, ((0, 8), (1, 4))),
    }


def block_ref(h_in, gain, proj, outw, coef, pair, delta):
    hf = h_in.astype(jnp.float32)
    normed = (hf * lax.rsqrt(lax.optimization_barrier(jnp.mean(hf * hf, -1, keepdims=True)) + 1e-06) * gain.astype(jnp.float32)).astype(jnp.bfloat16)
    query = jnp.dot(normed, proj[:, :D], preferred_element_type=jnp.float32).astype(jnp.bfloat16)
    keyval = jnp.dot(normed, proj[:, D:], preferred_element_type=jnp.float32).astype(jnp.bfloat16)
    query3 = query.astype(jnp.float32).reshape(ATOMS, HEADS, HEAD_DIM)
    keys = keyval[:, :D].astype(jnp.float32).reshape(ATOMS, HEADS, HEAD_DIM)
    values = keyval[:, D:].astype(jnp.float32).reshape(ATOMS, HEADS, HEAD_DIM)
    scores = jnp.einsum('ahd,jhd->haj', query3, keys) / math.sqrt(HEAD_DIM)
    weights = jax.nn.sigmoid(scores) * pair[None]
    rounded = lax.optimization_barrier(weights.astype(jnp.bfloat16)).astype(jnp.float32)
    message = (jnp.einsum('haj,jhd->ahd', rounded, values) / NBR).reshape(ATOMS, D).astype(jnp.bfloat16)
    h_out = (hf + jnp.dot(message, outw, preferred_element_type=jnp.float32)).astype(jnp.bfloat16)
    pair_coef = jnp.einsum('h,haj->aj', coef.astype(jnp.float32), weights)
    force = jnp.einsum('aj,caj->ca', pair_coef, delta) / NBR
    return (h_out, force)

def frame_pairs(nbr, mask, pos):
    rows = jnp.broadcast_to(jnp.arange(ATOMS, dtype=jnp.int32)[:, None], (ATOMS, NBR))
    counts = jnp.zeros((ATOMS, ATOMS), jnp.float32).at[rows, nbr].add(mask.astype(jnp.float32))
    delta = pos[:, None, :] - pos[:, :, None]
    switch = 1.0 / (1.0 + 0.125 * lax.optimization_barrier(jnp.sum(delta * delta, 0)))
    return (counts * switch, delta)

def reference(positions, atom_types, neighbors, nbr_mask, type_table, norm_gain, proj_weight, out_weight, force_coef):

    def member_forces(member):

        def frame_force(frame):
            pair, delta = frame_pairs(neighbors[frame], nbr_mask[frame], positions[frame])
            h_cur = jnp.take(type_table[member], atom_types[frame], axis=0)
            total = jnp.zeros((3, ATOMS), jnp.float32)
            for blk in range(SECTIONS):
                h_cur, term = block_ref(h_cur, norm_gain[member, blk], proj_weight[member, blk], out_weight[member, blk], force_coef[member, blk], pair, delta)
                total = total + term
            return total
        return lax.map(frame_force, jnp.arange(MICRO, dtype=jnp.int32))
    forces = lax.map(member_forces, jnp.arange(MEMBERS, dtype=jnp.int32))
    mean_force = lax.optimization_barrier(jnp.mean(forces, 0))
    centered = forces - mean_force[None]
    atom_dev = jnp.sqrt(lax.optimization_barrier(jnp.mean(lax.optimization_barrier(jnp.sum(centered * centered, 2)), 0)))
    max_dev = lax.optimization_barrier(jnp.max(atom_dev, -1))
    return (atom_dev, max_dev, mean_force)
```

```python
import functools
import math

import jax
import jax.numpy as jnp
from jax import lax
from jax.experimental import pallas as pl
from jax.experimental.pallas import tpu as pltpu
from jax.sharding import PartitionSpec as P

F32 = jnp.float32
BF16 = jnp.bfloat16
NT = (((1,), (1,)), ((), ()))


def kernel(
    dims,
    pos_hbm,
    types_hbm,
    nbr_hbm,
    mask_hbm,
    table_hbm,
    gain_hbm,
    proj_hbm,
    outw_hbm,
    coef_hbm,
    dev_out,
    max_out,
    mean_out,
    pos_in,
    types_in,
    nbr_in,
    mask_in,
    table,
    gain_in,
    coef_in,
    pack_src,
    packs,
    code_own,
    code_src,
    code_got,
    gc_src,
    gcs,
    projs,
    outs,
    counts,
    half_pair,
    coef_sum,
    xs,
    x_first,
    kv,
    qm,
    acc,
    hs,
    f_src,
    f_all,
    d_src,
    d_all,
    in_sem,
    own_sem,
    pack_ss,
    pack_rs,
    code_ss,
    code_rs,
    w_ss,
    w_rs,
    x_ss,
    x_rs,
    f_ss,
    f_rs,
    d_ss,
    d_rs,
):
    n_member, n_section, n_y, heads, head_dim, slots = dims
    width = heads * head_dim
    n_atoms = 2 * n_y
    blk = 128
    rows = 2 * blk
    me = lax.axis_index("member")
    sec = lax.axis_index("section")
    at = lax.axis_index("atoms")
    y = at // 2
    zh = at % 2
    other = 1 - zh
    at_other = 2 * y + other

    frames2 = pl.ds(2 * sec, 2)
    loads = [
        pltpu.make_async_copy(nbr_hbm.at[frames2], nbr_in, in_sem.at[0]),
        pltpu.make_async_copy(mask_hbm.at[frames2], mask_in, in_sem.at[1]),
        pltpu.make_async_copy(pos_hbm.at[frames2], pos_in, in_sem.at[2]),
        pltpu.make_async_copy(types_hbm, types_in, in_sem.at[3]),
        pltpu.make_async_copy(gain_hbm, gain_in, in_sem.at[4]),
        pltpu.make_async_copy(coef_hbm, coef_in, in_sem.at[5]),
        pltpu.make_async_copy(table_hbm, table, in_sem.at[6]),
    ]
    own_w = [
        pltpu.make_async_copy(proj_hbm.at[0, 0], projs.at[sec], own_sem.at[0]),
        pltpu.make_async_copy(outw_hbm.at[0, 0], outs.at[sec], own_sem.at[1]),
    ]
    for c in loads + own_w:
        c.start()

    atom_peers = []
    for k in range(n_y):
        y2 = (y + k) % n_y
        if k:
            atom_peers.append((2 * y2 + zh, zh))
        atom_peers.append((2 * y2 + other, other))
    ring = [k for k in (1, n_y - 1, 2) if k < n_y]
    ring = list(dict.fromkeys(ring))
    sec_peers = [(sec + k) % n_section for k in dict.fromkeys((1, n_section - 1, 2))]
    same_side = [(me + k) % n_member for k in range(1, n_member)]
    far_side = [(me + k) % n_member for k in range(n_member)]

    barrier = pltpu.get_barrier_semaphore()
    n_partners = 0

    def greet(device):
        pl.semaphore_signal(barrier, inc=1, device_id=device, device_id_type=pl.DeviceIdType.MESH)

    for a2, _ in atom_peers[1:]:
        greet({"atoms": a2})
        n_partners += 1
    for s2 in sec_peers:
        greet({"section": s2})
        n_partners += 1
    for m2 in same_side:
        greet({"member": m2})
        n_partners += 1
    for m2 in far_side:
        greet({"member": m2, "atoms": at_other})
        n_partners += 1
    pl.semaphore_wait(barrier, n_partners)

    def remote(src, dst, ss, rs, device):
        return pltpu.make_async_remote_copy(
            src_ref=src,
            dst_ref=dst,
            send_sem=ss,
            recv_sem=rs,
            device_id=device,
            device_id_type=pl.DeviceIdType.MESH,
        )

    sent = []

    def send(*what):
        copy = remote(*what)
        copy.start()
        sent.append(copy)

    def got(dst, rs):
        remote(dst, dst, x_ss.at[0, 0, 0], rs, {"section": sec_peers[0]}).wait_recv()

    loads[0].wait()
    loads[1].wait()
    unused = rows * n_y
    code_src[...] = nbr_in[other] + jnp.where(mask_in[other] != 0, 0, unused)
    z_lo = me // 2
    mirror = (n_member // 2 - 1 - z_lo) * 2 + me % 2
    send(code_src, code_got, code_ss, code_rs, {"member": mirror, "atoms": at_other})

    loads[2].wait()
    loads[3].wait()
    pack_src[...] = jnp.zeros_like(pack_src)
    for z in range(2):
        pack_src[z, 0:3, :] = pos_in[z]
        pack_src[z, 3:4, :] = types_in[pl.ds(2 * sec + z, 1), :].astype(F32)
    packs[at] = pack_src[zh]
    for n, (a2, z2) in enumerate(atom_peers):
        send(pack_src.at[z2], packs.at[at], pack_ss.at[n], pack_rs.at[at], {"atoms": a2})

    loads[4].wait()
    loads[5].wait()
    gc_src[...] = jnp.zeros_like(gc_src)
    gc_src[0:1, :] = gain_in[0].astype(F32)
    gc_src[1:2, 0:heads] = coef_in[0].astype(F32)
    gcs[sec] = gc_src[...]
    for n, s2 in enumerate(sec_peers):
        to = {"section": s2}
        send(gc_src, gcs.at[sec], w_ss.at[0, n], w_rs.at[0, sec], to)
        send(proj_hbm.at[0, 0], projs.at[sec], w_ss.at[1, n], w_rs.at[1, sec], to)
        send(outw_hbm.at[0, 0], outs.at[sec], w_ss.at[2, n], w_rs.at[2, sec], to)

    code_own[...] = nbr_in[zh] + jnp.where(mask_in[zh] != 0, 0, unused)

    iota_hi = lax.broadcasted_iota(jnp.int32, (8, blk), 0)
    iota_lo = lax.broadcasted_iota(jnp.int32, (blk, blk), 0)
    none = jnp.zeros((8, blk), F32)

    def count(code_ref, first_row):
        def group(g, carry):
            code = code_ref[pl.ds(pl.multiple_of(g * 8, 8), 8), :]
            hi = lax.shift_right_logical(code, 7)
            lo = jnp.bitwise_and(code, blk - 1)
            for r in range(0, 8, 2):
                left = [jnp.where(iota_hi == hi[r + e : r + e + 1, :], 1.0, 0.0).astype(F32) for e in (0, 1)]
                lhs = jnp.concatenate(
                    [
                        jnp.concatenate([left[0], none], axis=1),
                        jnp.concatenate([none, left[1]], axis=1),
                    ],
                    axis=0,
                ).astype(BF16)
                rhs = jnp.concatenate(
                    [
                        jnp.where(iota_lo == lo[r + e : r + e + 1, :], 1.0, 0.0).astype(BF16)
                        for e in (0, 1)
                    ],
                    axis=1,
                )
                both = lax.dot_general(lhs, rhs, NT, preferred_element_type=F32)
                counts[pl.ds(pl.multiple_of((first_row + g * 8 + r) * 8, 8), 16), :] = both
            return carry

        lax.fori_loop(0, blk // 8, group, 0)

    count(code_own, zh * blk)

    for a2, _ in atom_peers:
        got(packs.at[a2], pack_rs.at[a2])
    got(code_got, code_rs)
    count(code_got, other * blk)

    own_cols = [jnp.transpose(packs[2 * y + r]) for r in range(2)]

    def pair_half(kb, carry):
        pj = packs[kb]
        c = kb // 2
        lanes = pl.ds(pl.multiple_of((kb % 2) * blk, blk), blk)
        for r in range(2):
            dist = jnp.zeros((blk, blk), F32)
            for d in range(3):
                delta = pj[d : d + 1, :] - own_cols[r][:, d : d + 1]
                dist = dist + delta * delta
            cnt = counts[pl.ds(r * blk * 8 + kb, blk, stride=8), :]
            half_pair[c, r * blk : (r + 1) * blk, lanes] = 0.5 * cnt / (1.0 + 0.125 * dist)
        return carry

    lax.fori_loop(0, n_atoms, pair_half, 0)

    def normed(hf, gain):
        return (hf * lax.rsqrt(jnp.mean(hf * hf, -1, keepdims=True) + 1e-06) * gain).astype(BF16)

    lane_head = lax.broadcasted_iota(jnp.int32, (blk, width), 1) // head_dim

    def queries(x, layer, r):
        q = jnp.dot(x, projs[layer, :, 0:width], preferred_element_type=F32)
        for h in range(heads):
            qm[r, h * blk : (h + 1) * blk, :] = jnp.where(lane_head == h, q, 0.0).astype(BF16)

    def weights_ready(layer):
        @pl.when(sec != layer)
        def _():
            got(gcs.at[layer], w_rs.at[0, layer])
            got(projs.at[layer], w_rs.at[1, layer])
            got(outs.at[layer], w_rs.at[2, layer])

    for c in own_w:
        c.wait()
    loads[6].wait()
    weights_ready(0)

    x_table = normed(table[0].astype(F32), gcs[0, 0:1, :])
    iota_type = lax.broadcasted_iota(jnp.int32, (blk, blk), 1).astype(F32)

    def first_rows(kb, carry):
        types = jnp.transpose(packs[kb])[:, 3:4]
        onehot = jnp.where(iota_type == types, 1.0, 0.0).astype(BF16)
        x = jnp.dot(onehot, x_table, preferred_element_type=F32).astype(BF16)
        x_first[kb // 2, pl.ds(pl.multiple_of((kb % 2) * blk, blk), blk), :] = x
        return carry

    lax.fori_loop(0, n_atoms, first_rows, 0)
    for r in range(2):
        onehot = jnp.where(iota_type == own_cols[r][:, 3:4], 1.0, 0.0).astype(BF16)
        hs[r] = jnp.dot(onehot, table[0], preferred_element_type=F32).astype(BF16)
        queries(x_first[y, r * blk : (r + 1) * blk, :], 0, r)

    to_tanh = 0.5 / math.sqrt(head_dim)

    def unit(layer, r, c):
        last = layer == n_section - 1
        here = slice(r * blk, (r + 1) * blk)
        s = lax.dot_general(qm[r], kv[c, :, 0:width], NT, preferred_element_type=F32)
        half = half_pair[c, here, :]
        total = None
        gated = []
        for h in range(heads):
            t = jnp.tanh(s[h * blk : (h + 1) * blk, :] * to_tanh)
            term = gcs[layer, 1:2, h : h + 1] * t
            total = term if total is None else total + term
            if not last:
                gated.append((half * t + half).astype(BF16))
        if layer == 0:
            coef_sum[c, here, :] = total
        else:
            coef_sum[c, here, :] += total
        if not last:
            acc[r] += jnp.dot(
                jnp.concatenate(gated, axis=0), kv[c, :, width:], preferred_element_type=F32
            )

    def ring_chunk(j):
        return (y + j + (j // 2) * (1 - 2 * (j % 2))) % n_y

    for layer in range(n_section):
        last = layer == n_section - 1
        for r in range(2):
            if not last:
                acc[r] = jnp.zeros_like(acc[r])

            def step(j, carry):
                c = ring_chunk(j)
                if r == 0:
                    if layer == 0:
                        x = x_first[c]
                    else:

                        @pl.when(j > 0)
                        def _():
                            for e in range(2):
                                got(
                                    xs.at[layer - 1, c, e * blk : (e + 1) * blk],
                                    x_rs.at[layer - 1, e, c],
                                )

                        x = xs[layer - 1, c]
                    n_kv = width if last else 2 * width
                    kv[c, :, 0:n_kv] = jnp.dot(
                        x, projs[layer, :, width : width + n_kv], preferred_element_type=F32
                    ).astype(BF16)
                unit(layer, r, c)
                return carry

            lax.fori_loop(0, n_y, step, 0)
            if last:
                continue
            if r == 0:
                weights_ready(layer + 1)
            message = jnp.zeros((blk, width), F32)
            for h in range(heads):
                message = message + jnp.where(
                    lane_head == h, acc[r, h * blk : (h + 1) * blk, :], 0.0
                )
            message = (message * (1.0 / slots)).astype(BF16)
            h_new = (
                hs[r].astype(F32) + jnp.dot(message, outs[layer], preferred_element_type=F32)
            ).astype(BF16)
            hs[r] = h_new
            x = normed(h_new.astype(F32), gcs[layer + 1, 0:1, :])
            part = xs.at[layer, y, r * blk : (r + 1) * blk]
            part[...] = x
            for n, k in enumerate(ring):
                send(
                    part,
                    part,
                    x_ss.at[layer, r, n],
                    x_rs.at[layer, r, y],
                    {"atoms": 2 * ((y + k) % n_y) + zh},
                )
            queries(x, layer + 1, r)

    coef_all = jnp.zeros((1, 1), F32)
    for layer in range(n_section):
        coef_all = coef_all + jnp.sum(gcs[layer, 1:2, :], axis=1, keepdims=True)
    column = lax.broadcasted_iota(jnp.int32, (blk, 8), 1)
    for r in range(2):

        def force(kb, carry):
            pj = packs[kb]
            c = kb // 2
            lanes = pl.ds(pl.multiple_of((kb % 2) * blk, blk), blk)
            here = slice(r * blk, (r + 1) * blk)
            pull = half_pair[c, here, lanes] * (coef_sum[c, here, lanes] + coef_all)
            return tuple(
                carry[d] + pull * (pj[d : d + 1, :] - own_cols[r][:, d : d + 1]) for d in range(3)
            )

        parts = lax.fori_loop(0, n_atoms, force, (jnp.zeros((blk, blk), F32),) * 3)
        tile = jnp.zeros((blk, 8), F32)
        for d in range(3):
            tile = jnp.where(column == d, jnp.sum(parts[d], axis=1, keepdims=True), tile)
        f_src[r] = jnp.transpose(tile) * (1.0 / slots)

    slot = zh * n_member + me
    f_all[slot] = f_src[zh]
    for n, m2 in enumerate(same_side):
        send(f_src.at[zh], f_all.at[slot], f_ss.at[n], f_rs.at[slot], {"member": m2})
    for n, m2 in enumerate(far_side):
        send(
            f_src.at[other],
            f_all.at[slot],
            f_ss.at[n_member + n],
            f_rs.at[slot],
            {"member": m2, "atoms": at_other},
        )
    for m2 in same_side:
        got(f_all.at[zh * n_member + m2], f_rs.at[zh * n_member + m2])
    for m2 in far_side:
        got(f_all.at[other * n_member + m2], f_rs.at[other * n_member + m2])

    devs = []
    for z in range(2):
        total = f_all[z * n_member]
        for m in range(1, n_member):
            total = total + f_all[z * n_member + m]
        mean = total * (1.0 / n_member)
        mean_out[z] = mean[0:3, :]
        square = jnp.zeros((8, blk), F32)
        for m in range(n_member):
            centered = f_all[z * n_member + m] - mean
            square = square + centered * centered
        devs.append(jnp.sqrt(jnp.sum(square, axis=0, keepdims=True) * (1.0 / n_member)))
    row = lax.broadcasted_iota(jnp.int32, (8, blk), 0)
    dev = jnp.where(row == 0, devs[0], jnp.where(row == 1, devs[1], 0.0))
    dev_out[...] = dev[0:2, :]
    d_src[...] = dev
    d_all[at] = dev
    for n, (a2, _) in enumerate(atom_peers):
        send(d_src, d_all.at[at], d_ss.at[n], d_rs.at[at], {"atoms": a2})
    for a2, _ in atom_peers:
        got(d_all.at[a2], d_rs.at[a2])
    top = d_all[0]
    for a2 in range(1, n_atoms):
        top = jnp.maximum(top, d_all[a2])
    for z in range(2):
        max_out[z] = jnp.max(top[z : z + 1, :])

    for copy in sent:
        copy.wait_send()


def shards(
    positions,
    atom_types,
    neighbors,
    nbr_mask,
    type_table,
    norm_gain,
    proj_weight,
    out_weight,
    force_coef,
):
    n_section = lax.axis_size("section")
    n_member = lax.axis_size("member")
    n_atoms = lax.axis_size("atoms")
    n_y = n_atoms // 2
    heads = force_coef.shape[2]
    width = type_table.shape[2]
    blk = atom_types.shape[1]
    slots = neighbors.shape[2]
    frames = atom_types.shape[0]
    rows = 2 * blk
    dims = (n_member, n_section, n_y, heads, width // heads, slots)
    dma = pltpu.SemaphoreType.DMA
    vmem = pltpu.VMEM
    scratch = [
        vmem((2, 3, blk), F32),
        vmem((frames, blk), jnp.int32),
        vmem((2, blk, slots), jnp.int32),
        vmem((2, blk, slots), jnp.int32),
        vmem(type_table.shape, BF16),
        vmem(norm_gain.shape, BF16),
        vmem(force_coef.shape, BF16),
        vmem((2, 8, blk), F32),
        vmem((n_atoms, 8, blk), F32),
        vmem((blk, slots), jnp.int32),
        vmem((blk, slots), jnp.int32),
        vmem((blk, slots), jnp.int32),
        vmem((8, width), F32),
        vmem((n_section, 8, width), F32),
        vmem((n_section, width, 3 * width), BF16),
        vmem((n_section, width, width), BF16),
        vmem((rows * 8, blk), F32),
        vmem((n_y, rows, rows), F32),
        vmem((n_y, rows, rows), F32),
        vmem((n_section - 1, n_y, rows, width), BF16),
        vmem((n_y, rows, width), BF16),
        vmem((n_y, rows, 2 * width), BF16),
        vmem((2, heads * blk, width), BF16),
        vmem((2, heads * blk, width), F32),
        vmem((2, blk, width), BF16),
        vmem((2, 8, blk), F32),
        vmem((2 * n_member, 8, blk), F32),
        vmem((8, blk), F32),
        vmem((n_atoms, 8, blk), F32),
        dma((7,)),
        dma((2,)),
        dma((n_atoms,)),
        dma((n_atoms,)),
        dma,
        dma,
        dma((3, n_section)),
        dma((3, n_section)),
        dma((n_section - 1, 2, n_y)),
        dma((n_section - 1, 2, n_y)),
        dma((2 * n_member,)),
        dma((2 * n_member,)),
        dma((n_atoms,)),
        dma((n_atoms,)),
    ]
    own_frames = frames // n_section
    atom_dev, max_dev, mean_force = pl.pallas_call(
        functools.partial(kernel, dims),
        out_shape=(
            jax.ShapeDtypeStruct((own_frames, blk), F32),
            jax.ShapeDtypeStruct((own_frames,), F32),
            jax.ShapeDtypeStruct((own_frames, 3, blk), F32),
        ),
        in_specs=[pl.BlockSpec(memory_space=pl.ANY)] * 9,
        out_specs=(
            pl.BlockSpec(memory_space=pltpu.VMEM),
            pl.BlockSpec(memory_space=pltpu.SMEM),
            pl.BlockSpec(memory_space=pltpu.VMEM),
        ),
        scratch_shapes=scratch,
        compiler_params=pltpu.CompilerParams(
            collective_id=0, has_side_effects=True, vmem_limit_bytes=40 * 1024 * 1024
        ),
        name="committee",
    )(
        positions,
        atom_types,
        neighbors,
        nbr_mask,
        type_table,
        norm_gain,
        proj_weight,
        out_weight,
        force_coef,
    )
    return (atom_dev, max_dev, mean_force)


def solution(mesh):
    return jax.shard_map(
        shards,
        mesh=mesh,
        in_specs=(
            P(None, None, "atoms"),
            P(None, "atoms"),
            P(None, "atoms", None),
            P(None, "atoms", None),
            P("member", None, None),
            P("member", "section", None),
            P("member", "section", None, None),
            P("member", "section", None, None),
            P("member", "section", None),
        ),
        out_specs=(P("section", "atoms"), P("section"), P("section", None, "atoms")),
        check_vma=False,
    )
```

```python
import functools
import math

import jax
import jax.numpy as jnp
from jax import lax
from jax.experimental import pallas as pl
from jax.experimental.pallas import tpu as pltpu
from jax.sharding import PartitionSpec as P

F32 = jnp.float32
BF16 = jnp.bfloat16
NT = (((1,), (1,)), ((), ()))


def kernel(
    dims,
    pos_hbm,
    types_hbm,
    nbr_hbm,
    mask_hbm,
    table_hbm,
    gain_hbm,
    proj_hbm,
    outw_hbm,
    coef_hbm,
    result,
    pos_in,
    types_in,
    nbr_in,
    mask_in,
    table,
    gain_in,
    coef_in,
    pack_src,
    packs,
    code_own,
    code_src,
    code_got,
    gc_src,
    gcs,
    projs,
    outs,
    counts,
    half_pair,
    coef_sum,
    xs,
    kv,
    qm,
    acc,
    hs,
    f_all,
    d_all,
    in_sem,
    pack_ss,
    pack_rs,
    code_ss,
    code_rs,
    w_ss,
    w_rs,
    x_ss,
    x_rs,
    f_ss,
    f_rs,
    d_ss,
    d_rs,
):
    n_member, n_section, n_y, heads, head_dim, slots = dims
    width = heads * head_dim
    n_atoms = 2 * n_y
    blk = 128
    me = lax.axis_index("member")
    sec = lax.axis_index("section")
    at = lax.axis_index("atoms")
    y = at // 2
    zh = at % 2
    other = 1 - zh
    sides = (zh, other)
    mirror = (n_member // 2 - 1 - me // 2) * 2 + me % 2

    turns = list(dict.fromkeys(k for k in (1, n_y - 1, 2) if 0 < k < n_y))
    ring = [(y + k) % n_y for k in turns]
    near = [{"atoms": 2 * y2 + zh} for y2 in ring]
    across = [{"atoms": 2 * y2 + other, "member": mirror} for y2 in [y] + ring]
    sec_turns = list(dict.fromkeys((1, n_section - 1, 2)))
    sec_peers = [{"section": (sec + k) % n_section} for k in sec_turns]
    mates = [(me + k) % n_member for k in range(1, n_member)]

    barrier = pltpu.get_barrier_semaphore()
    partners = across + near + sec_peers + [{"member": m2} for m2 in mates]
    for device in partners:
        pl.semaphore_signal(barrier, inc=1, device_id=device, device_id_type=pl.DeviceIdType.MESH)

    frames2 = pl.ds(2 * sec, 2)
    loads = [
        pltpu.make_async_copy(nbr_hbm.at[frames2], nbr_in, in_sem.at[0]),
        pltpu.make_async_copy(mask_hbm.at[frames2], mask_in, in_sem.at[1]),
        pltpu.make_async_copy(pos_hbm, pos_in, in_sem.at[2]),
        pltpu.make_async_copy(types_hbm, types_in, in_sem.at[3]),
        pltpu.make_async_copy(gain_hbm, gain_in, in_sem.at[4]),
        pltpu.make_async_copy(coef_hbm, coef_in, in_sem.at[5]),
        pltpu.make_async_copy(proj_hbm.at[0, 0], projs.at[sec], in_sem.at[6]),
        pltpu.make_async_copy(outw_hbm.at[0, 0], outs.at[sec], in_sem.at[7]),
        pltpu.make_async_copy(table_hbm, table, in_sem.at[8]),
    ]
    for c in loads:
        c.start()

    def remote(src, dst, ss, rs, device):
        return pltpu.make_async_remote_copy(
            src_ref=src,
            dst_ref=dst,
            send_sem=ss,
            recv_sem=rs,
            device_id=device,
            device_id_type=pl.DeviceIdType.MESH,
        )

    sent = []

    def send(*what):
        copy = remote(*what)
        copy.start()
        sent.append(copy)

    def got(dst, rs):
        remote(dst, dst, x_ss.at[0, 0, 0], rs, sec_peers[0]).wait_recv()

    loads[0].wait()
    loads[1].wait()
    unused = n_atoms * blk
    code_src[...] = nbr_in[other] + jnp.where(mask_in[other] != 0, 0, unused)
    code_own[...] = nbr_in[zh] + jnp.where(mask_in[zh] != 0, 0, unused)

    loads[2].wait()
    loads[3].wait()
    pack_src[...] = jnp.zeros_like(pack_src)
    for r in range(2):
        frame = pl.ds(2 * sec + sides[r], 1)
        for d in range(3):
            pack_src[r, d : d + 1, :] = pos_in[d, frame, :]
        pack_src[r, 3:4, :] = types_in[frame, :].astype(F32)
    packs[at] = pack_src[0]
    loads[4].wait()
    loads[5].wait()
    gc_src[...] = jnp.zeros_like(gc_src)
    gc_src[0:1, :] = gain_in[0].astype(F32)
    gc_src[1:2, 0:heads] = coef_in[0].astype(F32)
    gcs[sec] = gc_src[...]

    pl.semaphore_wait(barrier, len(partners))
    send(code_src, code_got, code_ss, code_rs, across[0])
    for n, to in enumerate(near + across):
        r = 0 if n < len(near) else 1
        send(pack_src.at[r], packs.at[at], pack_ss.at[n], pack_rs.at[at], to)
    for n, to in enumerate(sec_peers):
        send(gc_src, gcs.at[sec], w_ss.at[0, n], w_rs.at[0, sec], to)
        send(proj_hbm.at[0, 0], projs.at[sec], w_ss.at[1, n], w_rs.at[1, sec], to)
        send(outw_hbm.at[0, 0], outs.at[sec], w_ss.at[2, n], w_rs.at[2, sec], to)

    iota_hi = lax.broadcasted_iota(jnp.int32, (8, blk), 0)
    iota_lo = lax.broadcasted_iota(jnp.int32, (blk, blk), 0)
    none = jnp.zeros((8, blk), F32)

    def count(code_ref, r):
        per = 16

        def group(g, carry):
            code = code_ref[pl.ds(pl.multiple_of(g * per, per), per), :]
            hi = lax.shift_right_logical(code, 7)
            lo = jnp.bitwise_and(code, blk - 1)
            for i in range(0, per, 2):
                left = [
                    jnp.where(iota_hi == hi[i + e : i + e + 1, :], 1.0, 0.0).astype(F32)
                    for e in (0, 1)
                ]
                lhs = jnp.concatenate(
                    [
                        jnp.concatenate([left[0], none], axis=1),
                        jnp.concatenate([none, left[1]], axis=1),
                    ],
                    axis=0,
                ).astype(BF16)
                rhs = jnp.concatenate(
                    [
                        jnp.where(iota_lo == lo[i + e : i + e + 1, :], 1.0, 0.0).astype(BF16)
                        for e in (0, 1)
                    ],
                    axis=1,
                )
                both = lax.dot_general(lhs, rhs, NT, preferred_element_type=F32)
                counts[pl.ds(pl.multiple_of((r * blk + g * per + i) * 8, 16), 16), :] = both
            return carry

        lax.fori_loop(0, blk // per, group, 0)

    count(code_own, 0)

    for y2 in ring:
        got(packs.at[2 * y2 + zh], pack_rs.at[2 * y2 + zh])
    for y2 in [y] + ring:
        got(packs.at[2 * y2 + other], pack_rs.at[2 * y2 + other])

    own_cols = [jnp.transpose(packs[2 * y + sides[r]]) for r in range(2)]

    def pair_half(r):
        for kb in range(n_atoms):
            pj = packs[kb]
            dist = jnp.zeros((blk, blk), F32)
            for d in range(3):
                delta = pj[d : d + 1, :] - own_cols[r][:, d : d + 1]
                dist = dist + delta * delta
            cnt = counts[pl.ds(r * blk * 8 + kb, blk, stride=8), :]
            half_pair[r, kb] = 0.5 * cnt / (1.0 + 0.125 * dist)

    pair_half(0)

    def normed(hf, gain):
        return (hf * lax.rsqrt(jnp.mean(hf * hf, -1, keepdims=True) + 1e-06) * gain).astype(BF16)

    lane_head = lax.broadcasted_iota(jnp.int32, (blk, width), 1) // head_dim

    def heads_apart(q, r):
        for h in range(heads):
            qm[r, h * blk : (h + 1) * blk, :] = jnp.where(lane_head == h, q, 0.0).astype(BF16)

    def queries(x, layer, r):
        heads_apart(jnp.dot(x, projs[layer, :, 0:width], preferred_element_type=F32), r)

    def keys(x, layer, kb):
        n_kv = width if layer == n_section - 1 else 2 * width
        kv[layer % 2, kb, :, 0:n_kv] = jnp.dot(
            x, projs[layer, :, width : width + n_kv], preferred_element_type=F32
        ).astype(BF16)

    def weights_ready(layer):
        @pl.when(sec != layer)
        def _():
            got(gcs.at[layer], w_rs.at[0, layer])
            got(projs.at[layer], w_rs.at[1, layer])
            got(outs.at[layer], w_rs.at[2, layer])

    for c in loads[6:]:
        c.wait()
    weights_ready(0)

    x_table = normed(table[0].astype(F32), gcs[0, 0:1, :])
    qkv_table = jnp.dot(x_table, projs[0], preferred_element_type=F32).astype(BF16)
    iota_type = lax.broadcasted_iota(jnp.int32, (blk, blk), 1).astype(F32)

    def onehot(columns):
        return jnp.where(iota_type == columns[:, 3:4], 1.0, 0.0).astype(BF16)

    for kb in range(n_atoms):
        kv[0, kb] = jnp.dot(
            onehot(jnp.transpose(packs[kb])), qkv_table[:, width:], preferred_element_type=F32
        ).astype(BF16)
    for r in range(2):
        which = onehot(own_cols[r])
        hs[r] = jnp.dot(which, table[0], preferred_element_type=F32).astype(BF16)
        heads_apart(jnp.dot(which, qkv_table[:, 0:width], preferred_element_type=F32), r)

    to_tanh = 0.5 / math.sqrt(head_dim)

    def unit(layer, r, blocks, first):
        last = layer == n_section - 1
        k = jnp.concatenate([kv[layer % 2, kb, :, 0:width] for kb in blocks], axis=0)
        s = lax.dot_general(qm[r], k, NT, preferred_element_type=F32)
        half = jnp.concatenate([half_pair[r, kb] for kb in blocks], axis=1)
        total = None
        gated = []
        for h in range(heads):
            t = jnp.tanh(s[h * blk : (h + 1) * blk, :] * to_tanh)
            term = gcs[layer, 1:2, h : h + 1] * t
            total = term if total is None else total + term
            if not last:
                gated.append((half * t + half).astype(BF16))
        for n, kb in enumerate(blocks):
            piece = total[:, n * blk : (n + 1) * blk]
            if layer == 0:
                coef_sum[r, kb] = piece
            else:
                coef_sum[r, kb] += piece
        if not last:
            v = jnp.concatenate([kv[layer % 2, kb, :, width:] for kb in blocks], axis=0)
            part = jnp.dot(jnp.concatenate(gated, axis=0), v, preferred_element_type=F32)
            if first:
                acc[r] = part
            else:
                acc[r] += part

    def finish(layer, r):
        message = acc[r, 0:blk, :]
        for h in range(1, heads):
            message = jnp.where(lane_head == h, acc[r, h * blk : (h + 1) * blk, :], message)
        message = (message * (1.0 / slots)).astype(BF16)
        h_new = (
            hs[r].astype(F32) + jnp.dot(message, outs[layer], preferred_element_type=F32)
        ).astype(BF16)
        hs[r] = h_new
        x = normed(h_new.astype(F32), gcs[layer + 1, 0:1, :])
        mine = 2 * y + sides[r]
        xs[layer, mine] = x
        part = xs.at[layer, mine]
        for n, to in enumerate(near):
            send(part, part, x_ss.at[layer, r, n], x_rs.at[layer, mine], to)
        queries(x, layer + 1, r)
        keys(x, layer + 1, mine)

    def arrived(layer, y2, r):
        kb = 2 * y2 + sides[r]
        got(xs.at[layer - 1, kb], x_rs.at[layer - 1, kb])
        keys(xs[layer - 1, kb], layer, kb)

    own_pair = (2 * y + zh, 2 * y + other)
    first_halves = [2 * y2 + zh for y2 in ring]
    second_halves = [2 * y2 + other for y2 in ring]
    rest = first_halves + second_halves
    groups = [own_pair] + [tuple(rest[i : i + 2]) for i in range(0, len(rest), 2)]

    for n, g in enumerate(groups):
        unit(0, 0, g, n == 0)
    weights_ready(1)
    finish(0, 0)
    got(code_got, code_rs)
    count(code_got, 1)
    pair_half(1)
    for n, g in enumerate(groups):
        unit(0, 1, g, n == 0)
    finish(0, 1)

    for layer in range(1, n_section):
        last = layer == n_section - 1
        for r in range(2):
            unit(layer, r, groups[0], True)
        for y2 in ring:
            arrived(layer, y2, 0)
        for r in range(2):
            unit(layer, r, groups[1], False)
        if not last:
            weights_ready(layer + 1)
        for y2 in ring:
            arrived(layer, y2, 1)
        for r in range(2):
            for g in groups[2:]:
                unit(layer, r, g, False)
            if not last:
                finish(layer, r)

    coef_all = jnp.zeros((1, 1), F32)
    for layer in range(n_section):
        coef_all = coef_all + jnp.sum(gcs[layer, 1:2, :], axis=1, keepdims=True)
    column = lax.broadcasted_iota(jnp.int32, (blk, 8), 1)
    tile = jnp.zeros((blk, 8), F32)
    for r in range(2):
        parts = [jnp.zeros((blk, blk), F32)] * 3
        for kb in range(n_atoms):
            pj = packs[kb]
            pull = half_pair[r, kb] * (coef_sum[r, kb] + coef_all)
            for d in range(3):
                parts[d] = parts[d] + pull * (pj[d : d + 1, :] - own_cols[r][:, d : d + 1])
        for d in range(3):
            tile = jnp.where(
                column == 4 * r + d, jnp.sum(parts[d], axis=1, keepdims=True), tile
            )
    f_all[me] = jnp.transpose(tile) * (1.0 / slots)
    for n, m2 in enumerate(mates):
        send(f_all.at[me], f_all.at[me], f_ss.at[n], f_rs.at[me], {"member": m2})
    for m2 in mates:
        got(f_all.at[m2], f_rs.at[m2])

    total = f_all[0]
    for m in range(1, n_member):
        total = total + f_all[m]
    mean = total * (1.0 / n_member)
    square = jnp.zeros((8, blk), F32)
    for m in range(n_member):
        centered = f_all[m] - mean
        square = square + centered * centered
    dev = [
        jnp.sqrt(jnp.sum(square[4 * r : 4 * r + 4], axis=0, keepdims=True) * (1.0 / n_member))
        for r in range(2)
    ]
    row = lax.broadcasted_iota(jnp.int32, (8, blk), 0)
    top = jnp.where(row == 4, jnp.maximum(dev[0], dev[1]), 0.0)
    mean_far = jnp.concatenate([mean[4:8], mean[0:4]], axis=0)
    d_all[at] = jnp.where(row < 3, mean_far, jnp.where(row == 3, dev[1], top))
    for n, to in enumerate(near + across):
        send(d_all.at[at], d_all.at[at], d_ss.at[n], d_rs.at[at], to)
    result[zh] = jnp.where(row < 3, mean, jnp.where(row == 3, dev[0], 0.0))
    for y2 in ring:
        got(d_all.at[2 * y2 + zh], d_rs.at[2 * y2 + zh])
    for y2 in [y] + ring:
        got(d_all.at[2 * y2 + other], d_rs.at[2 * y2 + other])
    result[other] = d_all[2 * y + other]
    for z in range(2):
        best = d_all[z]
        for y2 in range(1, n_y):
            best = jnp.maximum(best, d_all[2 * y2 + z])
        result[z, 4:5, :] = best[4:5, :]

    for copy in sent:
        copy.wait_send()


def finish_outputs(result, dev_out, max_out, mean_out):
    for z in range(2):
        for d in range(3):
            mean_out[d, z : z + 1, :] = result[z, d : d + 1, :]
        dev_out[z : z + 1, :] = result[z, 3:4, :]
        max_out[z] = jnp.max(result[z, 4:5, :])


def shards(
    positions,
    atom_types,
    neighbors,
    nbr_mask,
    type_table,
    norm_gain,
    proj_weight,
    out_weight,
    force_coef,
):
    n_section = lax.axis_size("section")
    n_member = lax.axis_size("member")
    n_atoms = lax.axis_size("atoms")
    n_y = n_atoms // 2
    heads = force_coef.shape[2]
    width = type_table.shape[2]
    blk = atom_types.shape[1]
    slots = neighbors.shape[2]
    frames = atom_types.shape[0]
    dims = (n_member, n_section, n_y, heads, width // heads, slots)
    dma = pltpu.SemaphoreType.DMA
    vmem = pltpu.VMEM
    scratch = [
        vmem((3, frames, blk), F32),
        vmem((frames, blk), jnp.int32),
        vmem((2, blk, slots), jnp.int32),
        vmem((2, blk, slots), jnp.int32),
        vmem(type_table.shape, BF16),
        vmem(norm_gain.shape, BF16),
        vmem(force_coef.shape, BF16),
        vmem((2, 8, blk), F32),
        vmem((n_atoms, 8, blk), F32),
        vmem((blk, slots), jnp.int32),
        vmem((blk, slots), jnp.int32),
        vmem((blk, slots), jnp.int32),
        vmem((8, width), F32),
        vmem((n_section, 8, width), F32),
        vmem((n_section, width, 3 * width), BF16),
        vmem((n_section, width, width), BF16),
        vmem((2 * blk * 8, blk), F32),
        vmem((2, n_atoms, blk, blk), F32),
        vmem((2, n_atoms, blk, blk), F32),
        vmem((n_section - 1, n_atoms, blk, width), BF16),
        vmem((2, n_atoms, blk, 2 * width), BF16),
        vmem((2, heads * blk, width), BF16),
        vmem((2, heads * blk, width), F32),
        vmem((2, blk, width), BF16),
        vmem((n_member, 8, blk), F32),
        vmem((n_atoms, 8, blk), F32),
        dma((9,)),
        dma((n_atoms,)),
        dma((n_atoms,)),
        dma,
        dma,
        dma((3, n_section)),
        dma((3, n_section)),
        dma((n_section - 1, 2, n_y)),
        dma((n_section - 1, n_atoms)),
        dma((n_member,)),
        dma((n_member,)),
        dma((n_atoms,)),
        dma((n_atoms,)),
    ]
    own_frames = frames // n_section
    result = pl.pallas_call(
        functools.partial(kernel, dims),
        out_shape=jax.ShapeDtypeStruct((own_frames, 8, blk), F32),
        in_specs=[pl.BlockSpec(memory_space=pltpu.HBM)] * 9,
        out_specs=pl.BlockSpec(memory_space=pltpu.VMEM),
        scratch_shapes=scratch,
        compiler_params=pltpu.CompilerParams(
            collective_id=0, has_side_effects=True, vmem_limit_bytes=56 * 1024 * 1024
        ),
        name="committee",
    )(
        jnp.transpose(positions, (1, 0, 2)),
        atom_types,
        neighbors,
        nbr_mask,
        type_table,
        norm_gain,
        proj_weight,
        out_weight,
        force_coef,
    )
    atom_dev, max_dev, mean_force = pl.pallas_call(
        finish_outputs,
        out_shape=(
            jax.ShapeDtypeStruct((own_frames, blk), F32),
            jax.ShapeDtypeStruct((own_frames,), F32),
            jax.ShapeDtypeStruct((3, own_frames, blk), F32),
        ),
        in_specs=[pl.BlockSpec(memory_space=pltpu.VMEM)],
        out_specs=(
            pl.BlockSpec(memory_space=pltpu.VMEM),
            pl.BlockSpec(memory_space=pltpu.SMEM),
            pl.BlockSpec(memory_space=pltpu.VMEM),
        ),
        name="outputs",
    )(result)
    return (atom_dev, max_dev, jnp.transpose(mean_force, (1, 0, 2)))


def solution(mesh):
    return jax.shard_map(
        shards,
        mesh=mesh,
        in_specs=(
            P(None, None, "atoms"),
            P(None, "atoms"),
            P(None, "atoms", None),
            P(None, "atoms", None),
            P("member", None, None),
            P("member", "section", None),
            P("member", "section", None, None),
            P("member", "section", None, None),
            P("member", "section", None),
        ),
        out_specs=(P("section", "atoms"), P("section"), P("section", None, "atoms")),
        check_vma=False,
    )
```

```python
import functools
import math

import jax
import jax.numpy as jnp
from jax import lax
from jax.experimental import pallas as pl
from jax.experimental.pallas import tpu as pltpu
from jax.sharding import PartitionSpec as P

F32 = jnp.float32
BF16 = jnp.bfloat16
NT = (((1,), (1,)), ((), ()))


def kernel(
    dims,
    pos_hbm,
    types_hbm,
    nbr_hbm,
    mask_hbm,
    table_hbm,
    gain_hbm,
    proj_hbm,
    outw_hbm,
    coef_hbm,
    dev_out,
    max_out,
    mean_out,
    pos_in,
    types_in,
    nbr_in,
    mask_in,
    table,
    gain_in,
    coef_in,
    pack_src,
    packs,
    code_own,
    code_src,
    code_got,
    gc_src,
    gcs,
    projs,
    outs,
    counts,
    half_pair,
    coef_sum,
    xs,
    kv,
    qm,
    acc,
    hs,
    f_all,
    d_all,
    in_sem,
    pack_ss,
    pack_rs,
    code_ss,
    code_rs,
    w_ss,
    w_rs,
    x_ss,
    x_rs,
    f_ss,
    f_rs,
    d_ss,
    d_rs,
):
    n_member, n_section, n_y, heads, head_dim, slots = dims
    width = heads * head_dim
    n_atoms = 2 * n_y
    blk = 128
    me = lax.axis_index("member")
    sec = lax.axis_index("section")
    at = lax.axis_index("atoms")
    y = at // 2
    zh = at % 2
    other = 1 - zh
    sides = (zh, other)
    mirror = (n_member // 2 - 1 - me // 2) * 2 + me % 2

    turns = list(dict.fromkeys(k for k in (1, n_y - 1, 2) if 0 < k < n_y))
    ring = [(y + k) % n_y for k in turns]
    near = [{"atoms": 2 * y2 + zh} for y2 in ring]
    across = [{"atoms": 2 * y2 + other, "member": mirror} for y2 in [y] + ring]
    sec_turns = list(dict.fromkeys((1, n_section - 1, 2)))
    sec_peers = [{"section": (sec + k) % n_section} for k in sec_turns]
    mates = [(me + k) % n_member for k in range(1, n_member)]

    barrier = pltpu.get_barrier_semaphore()
    partners = across + near + sec_peers + [{"member": m2} for m2 in mates]
    for device in partners:
        pl.semaphore_signal(barrier, inc=1, device_id=device, device_id_type=pl.DeviceIdType.MESH)

    frames2 = pl.ds(2 * sec, 2)
    loads = [
        pltpu.make_async_copy(pos_hbm, pos_in, in_sem.at[0]),
        pltpu.make_async_copy(types_hbm, types_in, in_sem.at[1]),
        pltpu.make_async_copy(nbr_hbm.at[frames2], nbr_in, in_sem.at[2]),
        pltpu.make_async_copy(mask_hbm.at[frames2], mask_in, in_sem.at[3]),
        pltpu.make_async_copy(gain_hbm, gain_in, in_sem.at[4]),
        pltpu.make_async_copy(coef_hbm, coef_in, in_sem.at[5]),
        pltpu.make_async_copy(proj_hbm.at[0, 0], projs.at[sec], in_sem.at[6]),
        pltpu.make_async_copy(outw_hbm.at[0, 0], outs.at[sec], in_sem.at[7]),
        pltpu.make_async_copy(table_hbm, table, in_sem.at[8]),
    ]
    for c in loads:
        c.start()

    def remote(src, dst, ss, rs, device):
        return pltpu.make_async_remote_copy(
            src_ref=src,
            dst_ref=dst,
            send_sem=ss,
            recv_sem=rs,
            device_id=device,
            device_id_type=pl.DeviceIdType.MESH,
        )

    sent = []

    def send(*what):
        copy = remote(*what)
        copy.start()
        sent.append(copy)

    def got(dst, rs):
        remote(dst, dst, x_ss.at[0, 0, 0], rs, sec_peers[0]).wait_recv()

    loads[0].wait()
    loads[1].wait()
    pack_src[...] = jnp.zeros_like(pack_src)
    for r in range(2):
        frame = pl.ds(2 * sec + sides[r], 1)
        for d in range(3):
            pack_src[r, d : d + 1, :] = pos_in[d, frame, :]
        pack_src[r, 3:4, :] = types_in[frame, :].astype(F32)
    packs[at] = pack_src[0]
    pl.semaphore_wait(barrier, len(partners))
    for n, to in enumerate(across):
        send(pack_src.at[1], packs.at[at], pack_ss.at[n], pack_rs.at[at], to)

    loads[2].wait()
    loads[3].wait()
    unused = n_atoms * blk
    code_src[...] = nbr_in[other] + jnp.where(mask_in[other] != 0, 0, unused)
    send(code_src, code_got, code_ss, code_rs, across[0])
    for n, to in enumerate(near):
        send(pack_src.at[0], packs.at[at], pack_ss.at[n_y + n], pack_rs.at[at], to)
    for n, to in enumerate(sec_peers):
        send(proj_hbm.at[0, 0], projs.at[sec], w_ss.at[1, n], w_rs.at[1, sec], to)
    loads[4].wait()
    loads[5].wait()
    gc_src[...] = jnp.zeros_like(gc_src)
    gc_src[0:1, :] = gain_in[0].astype(F32)
    gc_src[1:2, 0:heads] = coef_in[0].astype(F32)
    gcs[sec] = gc_src[...]
    for n, to in enumerate(sec_peers):
        send(gc_src, gcs.at[sec], w_ss.at[0, n], w_rs.at[0, sec], to)
    for n, to in enumerate(sec_peers):
        send(outw_hbm.at[0, 0], outs.at[sec], w_ss.at[2, n], w_rs.at[2, sec], to)
    code_own[...] = nbr_in[zh] + jnp.where(mask_in[zh] != 0, 0, unused)

    iota_hi = lax.broadcasted_iota(jnp.int32, (8, blk), 0)
    iota_lo = lax.broadcasted_iota(jnp.int32, (blk, blk), 0)
    none = jnp.zeros((8, blk), F32)

    def count(code_ref, r):
        code = code_ref[...]
        hi = lax.shift_right_logical(code, 7)
        lo = jnp.bitwise_and(code, blk - 1)
        for i in range(0, blk, 2):
            left = [
                jnp.where(iota_hi == hi[i + e : i + e + 1, :], 1.0, 0.0).astype(F32)
                for e in (0, 1)
            ]
            lhs = jnp.concatenate(
                [
                    jnp.concatenate([left[0], none], axis=1),
                    jnp.concatenate([none, left[1]], axis=1),
                ],
                axis=0,
            ).astype(BF16)
            rhs = jnp.concatenate(
                [
                    jnp.where(iota_lo == lo[i + e : i + e + 1, :], 1.0, 0.0).astype(BF16)
                    for e in (0, 1)
                ],
                axis=1,
            )
            both = lax.dot_general(lhs, rhs, NT, preferred_element_type=F32)
            first_row = (r * blk + i) * 8
            counts[first_row : first_row + 16, :] = both

    count(code_own, 0)

    near_blocks = [2 * y2 + zh for y2 in [y] + ring]
    far_blocks = [2 * y2 + other for y2 in [y] + ring]

    def pair_half(r, cols, blocks):
        for kb in blocks:
            pj = packs[kb]
            dist = jnp.zeros((blk, blk), F32)
            for d in range(3):
                delta = pj[d : d + 1, :] - cols[:, d : d + 1]
                dist = dist + delta * delta
            cnt = counts[pl.ds(r * blk * 8 + kb, blk, stride=8), :]
            half_pair[r, kb] = 0.5 * cnt / (1.0 + 0.125 * dist)

    def normed(hf, gain):
        return (hf * lax.rsqrt(jnp.mean(hf * hf, -1, keepdims=True) + 1e-06) * gain).astype(BF16)

    lane_head = lax.broadcasted_iota(jnp.int32, (blk, width), 1) // head_dim

    def heads_apart(q, r):
        for h in range(heads):
            qm[r, h * blk : (h + 1) * blk, :] = jnp.where(lane_head == h, q, 0.0).astype(BF16)

    def queries(x, layer, r):
        heads_apart(jnp.dot(x, projs[layer, :, 0:width], preferred_element_type=F32), r)

    def keys(x, layer, blocks):
        n_kv = width if layer == n_section - 1 else 2 * width
        out = jnp.dot(
            x, projs[layer, :, width : width + n_kv], preferred_element_type=F32
        ).astype(BF16)
        for n, kb in enumerate(blocks):
            kv[layer % 2, kb, :, 0:n_kv] = out[n * blk : (n + 1) * blk]

    def weights_ready(layer):
        @pl.when(sec != layer)
        def _():
            got(gcs.at[layer], w_rs.at[0, layer])
            got(projs.at[layer], w_rs.at[1, layer])
            got(outs.at[layer], w_rs.at[2, layer])

    for c in loads[6:]:
        c.wait()
    weights_ready(0)

    x_table = normed(table[0].astype(F32), gcs[0, 0:1, :])
    qkv_table = jnp.dot(x_table, projs[0], preferred_element_type=F32).astype(BF16)
    iota_type = lax.broadcasted_iota(jnp.int32, (blk, blk), 1).astype(F32)

    def onehot(columns):
        return jnp.where(iota_type == columns[:, 3:4], 1.0, 0.0).astype(BF16)

    def first_keys(blocks):
        for kb in blocks:
            kv[0, kb] = jnp.dot(
                onehot(jnp.transpose(packs[kb])), qkv_table[:, width:], preferred_element_type=F32
            ).astype(BF16)

    def first_rows(cols, r):
        which = onehot(cols)
        hs[r] = jnp.dot(which, table[0], preferred_element_type=F32).astype(BF16)
        heads_apart(jnp.dot(which, qkv_table[:, 0:width], preferred_element_type=F32), r)

    to_tanh = 0.5 / math.sqrt(head_dim)

    def unit(layer, r, blocks, first):
        last = layer == n_section - 1
        k = jnp.concatenate([kv[layer % 2, kb, :, 0:width] for kb in blocks], axis=0)
        s = lax.dot_general(qm[r], k, NT, preferred_element_type=F32)
        half = jnp.concatenate([half_pair[r, kb] for kb in blocks], axis=1)
        total = None
        gated = []
        for h in range(heads):
            t = jnp.tanh(s[h * blk : (h + 1) * blk, :] * to_tanh)
            term = gcs[layer, 1:2, h : h + 1] * t
            total = term if total is None else total + term
            if not last:
                gated.append((half * t + half).astype(BF16))
        for n, kb in enumerate(blocks):
            piece = total[:, n * blk : (n + 1) * blk]
            if layer == 0:
                coef_sum[r, kb] = piece
            else:
                coef_sum[r, kb] += piece
        if not last:
            v = jnp.concatenate([kv[layer % 2, kb, :, width:] for kb in blocks], axis=0)
            part = jnp.dot(jnp.concatenate(gated, axis=0), v, preferred_element_type=F32)
            if first:
                acc[r] = part
            else:
                acc[r] += part

    def finish(layer, r):
        message = acc[r, 0:blk, :]
        for h in range(1, heads):
            message = jnp.where(lane_head == h, acc[r, h * blk : (h + 1) * blk, :], message)
        message = (message * (1.0 / slots)).astype(BF16)
        h_new = (
            hs[r].astype(F32) + jnp.dot(message, outs[layer], preferred_element_type=F32)
        ).astype(BF16)
        hs[r] = h_new
        x = normed(h_new.astype(F32), gcs[layer + 1, 0:1, :])
        mine = 2 * y + sides[r]
        xs[layer, mine] = x
        part = xs.at[layer, mine]
        for n, to in reversed(list(enumerate(near))):
            send(part, part, x_ss.at[layer, r, n], x_rs.at[layer, mine], to)

    def prepare(layer):
        own = [xs[layer, 2 * y + sides[r]] for r in range(2)]
        for r in range(2):
            queries(own[r], layer + 1, r)
        keys(jnp.concatenate(own, axis=0), layer + 1, [2 * y + zh, 2 * y + other])

    def arrived(layer, r):
        blocks = [2 * y2 + sides[r] for y2 in ring]
        for kb in blocks:
            got(xs.at[layer - 1, kb], x_rs.at[layer - 1, kb])
        keys(jnp.concatenate([xs[layer - 1, kb] for kb in blocks], axis=0), layer, blocks)

    for y2 in ring:
        got(packs.at[2 * y2 + zh], pack_rs.at[2 * y2 + zh])
    cols_own = jnp.transpose(packs[at])
    pair_half(0, cols_own, near_blocks)
    first_keys(near_blocks)
    first_rows(cols_own, 0)
    unit(0, 0, near_blocks, True)
    for kb in far_blocks:
        got(packs.at[kb], pack_rs.at[kb])
    cols_far = jnp.transpose(packs[2 * y + other])
    own_cols = [cols_own, cols_far]
    pair_half(0, cols_own, far_blocks)
    first_keys(far_blocks)
    first_rows(cols_far, 1)
    unit(0, 0, far_blocks, False)
    weights_ready(1)
    finish(0, 0)
    got(code_got, code_rs)
    count(code_got, 1)
    pair_half(1, cols_far, near_blocks + far_blocks)
    unit(0, 1, near_blocks, True)
    unit(0, 1, far_blocks, False)
    finish(0, 1)
    prepare(0)

    for layer in range(1, n_section):
        last = layer == n_section - 1
        for r in range(2):
            unit(layer, r, [2 * y + zh, 2 * y + other], True)
        arrived(layer, 0)
        for r in range(2):
            unit(layer, r, near_blocks[1:], False)
        if not last:
            weights_ready(layer + 1)
        arrived(layer, 1)
        for r in range(2):
            unit(layer, r, far_blocks[1:], False)
            if not last:
                finish(layer, r)
        if not last:
            prepare(layer)

    coef_all = jnp.zeros((1, 1), F32)
    for layer in range(n_section):
        coef_all = coef_all + jnp.sum(gcs[layer, 1:2, :], axis=1, keepdims=True)
    column = lax.broadcasted_iota(jnp.int32, (blk, 8), 1)
    tile = jnp.zeros((blk, 8), F32)
    for r in range(2):
        parts = [jnp.zeros((blk, blk), F32)] * 3
        for kb in range(n_atoms):
            pj = packs[kb]
            pull = half_pair[r, kb] * (coef_sum[r, kb] + coef_all)
            for d in range(3):
                parts[d] = parts[d] + pull * (pj[d : d + 1, :] - own_cols[r][:, d : d + 1])
        for d in range(3):
            tile = jnp.where(
                column == 4 * r + d, jnp.sum(parts[d], axis=1, keepdims=True), tile
            )
    f_all[me] = jnp.transpose(tile) * (1.0 / slots)
    for n, m2 in enumerate(mates):
        send(f_all.at[me], f_all.at[me], f_ss.at[n], f_rs.at[me], {"member": m2})
    for m2 in mates:
        got(f_all.at[m2], f_rs.at[m2])

    total = f_all[0]
    for m in range(1, n_member):
        total = total + f_all[m]
    mean = total * (1.0 / n_member)
    square = jnp.zeros((8, blk), F32)
    for m in range(n_member):
        centered = f_all[m] - mean
        square = square + centered * centered
    dev = [
        jnp.sqrt(jnp.sum(square[4 * r : 4 * r + 4], axis=0, keepdims=True) * (1.0 / n_member))
        for r in range(2)
    ]
    row = lax.broadcasted_iota(jnp.int32, (8, blk), 0)
    top = jnp.where(row == 4, jnp.maximum(dev[0], dev[1]), 0.0)
    mean_far = jnp.concatenate([mean[4:8], mean[0:4]], axis=0)
    d_all[at] = jnp.where(row < 3, mean_far, jnp.where(row == 3, dev[1], top))
    for n, to in enumerate(near + across):
        send(d_all.at[at], d_all.at[at], d_ss.at[n], d_rs.at[at], to)
    for y2 in ring:
        got(d_all.at[2 * y2 + zh], d_rs.at[2 * y2 + zh])
    for y2 in [y] + ring:
        got(d_all.at[2 * y2 + other], d_rs.at[2 * y2 + other])
    far = d_all[2 * y + other]
    first = zh == 0
    dev_out[0:1, :] = jnp.where(first, dev[0], far[3:4, :])
    dev_out[1:2, :] = jnp.where(first, far[3:4, :], dev[0])
    for d in range(3):
        mean_out[d, 0:1, :] = jnp.where(first, mean[d : d + 1, :], far[d : d + 1, :])
        mean_out[d, 1:2, :] = jnp.where(first, far[d : d + 1, :], mean[d : d + 1, :])
    for z in range(2):
        best = d_all[z]
        for y2 in range(1, n_y):
            best = jnp.maximum(best, d_all[2 * y2 + z])
        max_out[z] = jnp.max(best[4:5, :])

    for copy in sent:
        copy.wait_send()


def hand_on(dev_in, max_in, mean_in, dev_out, max_out, mean_out, sem):
    copies = [
        pltpu.make_async_copy(a, b, sem.at[n])
        for n, (a, b) in enumerate([(dev_in, dev_out), (max_in, max_out), (mean_in, mean_out)])
    ]
    for c in copies:
        c.start()
    for c in copies:
        c.wait()


def shards(
    positions,
    atom_types,
    neighbors,
    nbr_mask,
    type_table,
    norm_gain,
    proj_weight,
    out_weight,
    force_coef,
):
    n_section = lax.axis_size("section")
    n_member = lax.axis_size("member")
    n_atoms = lax.axis_size("atoms")
    n_y = n_atoms // 2
    heads = force_coef.shape[2]
    width = type_table.shape[2]
    blk = atom_types.shape[1]
    slots = neighbors.shape[2]
    frames = atom_types.shape[0]
    dims = (n_member, n_section, n_y, heads, width // heads, slots)
    dma = pltpu.SemaphoreType.DMA
    vmem = pltpu.VMEM
    scratch = [
        vmem((3, frames, blk), F32),
        vmem((frames, blk), jnp.int32),
        vmem((2, blk, slots), jnp.int32),
        vmem((2, blk, slots), jnp.int32),
        vmem(type_table.shape, BF16),
        vmem(norm_gain.shape, BF16),
        vmem(force_coef.shape, BF16),
        vmem((2, 8, blk), F32),
        vmem((n_atoms, 8, blk), F32),
        vmem((blk, slots), jnp.int32),
        vmem((blk, slots), jnp.int32),
        vmem((blk, slots), jnp.int32),
        vmem((8, width), F32),
        vmem((n_section, 8, width), F32),
        vmem((n_section, width, 3 * width), BF16),
        vmem((n_section, width, width), BF16),
        vmem((2 * blk * 8, blk), F32),
        vmem((2, n_atoms, blk, blk), F32),
        vmem((2, n_atoms, blk, blk), F32),
        vmem((n_section - 1, n_atoms, blk, width), BF16),
        vmem((2, n_atoms, blk, 2 * width), BF16),
        vmem((2, heads * blk, width), BF16),
        vmem((2, heads * blk, width), F32),
        vmem((2, blk, width), BF16),
        vmem((n_member, 8, blk), F32),
        vmem((n_atoms, 8, blk), F32),
        dma((9,)),
        dma((n_atoms,)),
        dma((n_atoms,)),
        dma,
        dma,
        dma((3, n_section)),
        dma((3, n_section)),
        dma((n_section - 1, 2, n_y)),
        dma((n_section - 1, n_atoms)),
        dma((n_member,)),
        dma((n_member,)),
        dma((n_atoms,)),
        dma((n_atoms,)),
    ]
    own_frames = frames // n_section
    results = (
        jax.ShapeDtypeStruct((own_frames, blk), F32),
        jax.ShapeDtypeStruct((own_frames,), F32),
        jax.ShapeDtypeStruct((3, own_frames, blk), F32),
    )
    made = pl.pallas_call(
        functools.partial(kernel, dims),
        out_shape=results,
        in_specs=[pl.BlockSpec(memory_space=pltpu.HBM)] * 9,
        out_specs=(
            pl.BlockSpec(memory_space=pltpu.VMEM),
            pl.BlockSpec(memory_space=pltpu.SMEM),
            pl.BlockSpec(memory_space=pltpu.VMEM),
        ),
        scratch_shapes=scratch,
        compiler_params=pltpu.CompilerParams(
            collective_id=0, has_side_effects=True, vmem_limit_bytes=56 * 1024 * 1024
        ),
        name="committee",
    )(
        jnp.transpose(positions, (1, 0, 2)),
        atom_types,
        neighbors,
        nbr_mask,
        type_table,
        norm_gain,
        proj_weight,
        out_weight,
        force_coef,
    )
    atom_dev, max_dev, mean_force = pl.pallas_call(
        hand_on,
        out_shape=results,
        in_specs=[pl.BlockSpec(memory_space=pl.ANY)] * 3,
        out_specs=(pl.BlockSpec(memory_space=pl.ANY),) * 3,
        scratch_shapes=[dma((3,))],
        name="outputs",
    )(*made)
    return (atom_dev, max_dev, jnp.transpose(mean_force, (1, 0, 2)))


def solution(mesh):
    return jax.shard_map(
        shards,
        mesh=mesh,
        in_specs=(
            P(None, None, "atoms"),
            P(None, "atoms"),
            P(None, "atoms", None),
            P(None, "atoms", None),
            P("member", None, None),
            P("member", "section", None),
            P("member", "section", None, None),
            P("member", "section", None, None),
            P("member", "section", None),
        ),
        out_specs=(P("section", "atoms"), P("section"), P("section", None, "atoms")),
        check_vma=False,
    )
```

```python
import functools
import math

import jax
import jax.numpy as jnp
from jax import lax
from jax.experimental import pallas as pl
from jax.experimental.pallas import tpu as pltpu
from jax.sharding import PartitionSpec as P

F32 = jnp.float32
BF16 = jnp.bfloat16
NT = (((1,), (1,)), ((), ()))


def kernel(
    dims,
    pos_hbm,
    types_hbm,
    nbr_hbm,
    mask_hbm,
    table_hbm,
    gain_hbm,
    proj_hbm,
    outw_hbm,
    coef_hbm,
    dev_out,
    max_out,
    mean_out,
    pos_in,
    types_in,
    nbr_in,
    mask_in,
    table,
    gain_in,
    coef_in,
    pack_src,
    packs,
    code_own,
    code_src,
    code_got,
    gc_src,
    gcs,
    projs,
    outs,
    counts,
    half_pair,
    coef_sum,
    xs,
    kv,
    qm,
    acc,
    hs,
    f_all,
    d_all,
    pulled,
    in_sem,
    pack_ss,
    pack_rs,
    code_ss,
    code_rs,
    w_ss,
    w_rs,
    x_ss,
    x_rs,
    f_ss,
    f_rs,
    d_ss,
    d_rs,
):
    n_member, n_section, n_y, heads, head_dim, slots = dims
    width = heads * head_dim
    n_atoms = 2 * n_y
    blk = 128
    me = lax.axis_index("member")
    sec = lax.axis_index("section")
    at = lax.axis_index("atoms")
    y = at // 2
    zh = at % 2
    other = 1 - zh
    sides = (zh, other)
    mirror = (n_member // 2 - 1 - me // 2) * 2 + me % 2

    turns = list(dict.fromkeys(k for k in (1, n_y - 1, 2) if 0 < k < n_y))
    ring = [(y + k) % n_y for k in turns]
    near = [{"atoms": 2 * y2 + zh} for y2 in ring]
    across = [{"atoms": 2 * y2 + other, "member": mirror} for y2 in [y] + ring]
    sec_turns = list(dict.fromkeys((1, n_section - 1, 2)))
    sec_peers = [{"section": (sec + k) % n_section} for k in sec_turns]
    mates = [(me + k) % n_member for k in range(1, n_member)]

    barrier = pltpu.get_barrier_semaphore()
    far_mates = [(me + k) % n_member for k in range(n_member)]
    partners = across[1:] + [{"member": m2, "atoms": 2 * y + other} for m2 in far_mates]
    partners = partners + near + sec_peers + [{"member": m2} for m2 in mates]
    n_far = n_y - 1 + n_member

    def greet(devices):
        for device in devices:
            pl.semaphore_signal(
                barrier, inc=1, device_id=device, device_id_type=pl.DeviceIdType.MESH
            )

    greet(partners[:n_far])

    frames2 = pl.ds(2 * sec, 2)
    loads = [
        pltpu.make_async_copy(pos_hbm, pos_in, in_sem.at[0]),
        pltpu.make_async_copy(types_hbm, types_in, in_sem.at[1]),
        pltpu.make_async_copy(nbr_hbm.at[frames2], nbr_in, in_sem.at[2]),
        pltpu.make_async_copy(mask_hbm.at[frames2], mask_in, in_sem.at[3]),
        pltpu.make_async_copy(gain_hbm, gain_in, in_sem.at[4]),
        pltpu.make_async_copy(coef_hbm, coef_in, in_sem.at[5]),
        pltpu.make_async_copy(proj_hbm.at[0, 0], projs.at[sec], in_sem.at[6]),
        pltpu.make_async_copy(outw_hbm.at[0, 0], outs.at[sec], in_sem.at[7]),
        pltpu.make_async_copy(table_hbm, table, in_sem.at[8]),
    ]
    for c in loads:
        c.start()
    greet(partners[n_far:])

    def remote(src, dst, ss, rs, device):
        return pltpu.make_async_remote_copy(
            src_ref=src,
            dst_ref=dst,
            send_sem=ss,
            recv_sem=rs,
            device_id=device,
            device_id_type=pl.DeviceIdType.MESH,
        )

    sent = []

    def send(*what):
        copy = remote(*what)
        copy.start()
        sent.append(copy)

    def all_left():
        while sent:
            sent.pop(0).wait_send()

    def got(dst, rs):
        remote(dst, dst, x_ss.at[0, 0, 0], rs, sec_peers[0]).wait_recv()

    loads[0].wait()
    loads[1].wait()
    pack_src[...] = jnp.zeros_like(pack_src)
    for r in range(2):
        frame = pl.ds(2 * sec + sides[r], 1)
        for d in range(3):
            pack_src[r, d : d + 1, :] = pos_in[d, frame, :]
        pack_src[r, 3:4, :] = types_in[frame, :].astype(F32)
    packs[at] = pack_src[0]
    pl.semaphore_wait(barrier, len(partners))
    for n, to in enumerate(across):
        send(pack_src.at[1], packs.at[at], pack_ss.at[n], pack_rs.at[at], to)

    loads[4].wait()
    loads[5].wait()
    gc_src[...] = jnp.zeros_like(gc_src)
    gc_src[0:1, :] = gain_in[0].astype(F32)
    gc_src[1:2, 0:heads] = coef_in[0].astype(F32)
    gcs[sec] = gc_src[...]
    shares = []
    for a, b, what in (
        (proj_hbm.at[0, 0], projs.at[sec], 1),
        (gc_src, gcs.at[sec], 0),
        (outw_hbm.at[0, 0], outs.at[sec], 2),
    ):
        for n, to in enumerate(sec_peers):
            shares.append(remote(a, b, w_ss.at[what, n], w_rs.at[what, sec], to))
    sent.extend(shares)

    def share(when):
        @pl.when(when)
        def _():
            for copy in shares:
                copy.start()

    share(sec == 0)

    loads[2].wait()
    loads[3].wait()
    unused = n_atoms * blk
    code_src[...] = nbr_in[other] + jnp.where(mask_in[other] != 0, 0, unused)
    send(code_src, code_got, code_ss, code_rs, across[0])
    for n, to in enumerate(near):
        send(pack_src.at[0], packs.at[at], pack_ss.at[n_y + n], pack_rs.at[at], to)
    code_own[...] = nbr_in[zh] + jnp.where(mask_in[zh] != 0, 0, unused)

    iota_hi = lax.broadcasted_iota(jnp.int32, (8, blk), 0)
    iota_lo = lax.broadcasted_iota(jnp.int32, (blk, blk), 0)
    none = jnp.zeros((8, blk), F32)

    def count(code_ref, r):
        code = code_ref[...]
        hi = lax.shift_right_logical(code, 7)
        lo = jnp.bitwise_and(code, blk - 1)
        for i in range(0, blk, 2):
            left = [
                jnp.where(iota_hi == hi[i + e : i + e + 1, :], 1.0, 0.0).astype(F32)
                for e in (0, 1)
            ]
            lhs = jnp.concatenate(
                [
                    jnp.concatenate([left[0], none], axis=1),
                    jnp.concatenate([none, left[1]], axis=1),
                ],
                axis=0,
            ).astype(BF16)
            rhs = jnp.concatenate(
                [
                    jnp.where(iota_lo == lo[i + e : i + e + 1, :], 1.0, 0.0).astype(BF16)
                    for e in (0, 1)
                ],
                axis=1,
            )
            both = lax.dot_general(lhs, rhs, NT, preferred_element_type=F32)
            first_row = (r * blk + i) * 8
            counts[first_row : first_row + 16, :] = both

    count(code_own, 0)
    share(sec != 0)

    near_blocks = [2 * y2 + zh for y2 in [y] + ring]
    far_blocks = [2 * y2 + other for y2 in [y] + ring]

    def pair_half(r, cols, blocks):
        for kb in blocks:
            pj = packs[kb]
            dist = jnp.zeros((blk, blk), F32)
            for d in range(3):
                delta = pj[d : d + 1, :] - cols[:, d : d + 1]
                dist = dist + delta * delta
            cnt = counts[pl.ds(r * blk * 8 + kb, blk, stride=8), :]
            half_pair[r, kb] = 0.5 * cnt / (1.0 + 0.125 * dist)

    def normed(hf, gain):
        return (hf * lax.rsqrt(jnp.mean(hf * hf, -1, keepdims=True) + 1e-06) * gain).astype(BF16)

    lane_head = lax.broadcasted_iota(jnp.int32, (blk, width), 1) // head_dim

    def heads_apart(q, r):
        for h in range(heads):
            qm[r, h * blk : (h + 1) * blk, :] = jnp.where(lane_head == h, q, 0.0).astype(BF16)

    def queries(x, layer, r):
        heads_apart(jnp.dot(x, projs[layer, :, 0:width], preferred_element_type=F32), r)

    def keys(x, layer, blocks):
        n_kv = width if layer == n_section - 1 else 2 * width
        out = jnp.dot(
            x, projs[layer, :, width : width + n_kv], preferred_element_type=F32
        ).astype(BF16)
        for n, kb in enumerate(blocks):
            kv[layer % 2, kb, :, 0:n_kv] = out[n * blk : (n + 1) * blk]

    def weights_ready(layer):
        @pl.when(sec != layer)
        def _():
            got(gcs.at[layer], w_rs.at[0, layer])
            got(projs.at[layer], w_rs.at[1, layer])
            got(outs.at[layer], w_rs.at[2, layer])

    for c in loads[6:]:
        c.wait()
    weights_ready(0)

    x_table = normed(table[0].astype(F32), gcs[0, 0:1, :])
    qkv_table = jnp.dot(x_table, projs[0], preferred_element_type=F32).astype(BF16)
    iota_type = lax.broadcasted_iota(jnp.int32, (blk, blk), 1).astype(F32)

    def onehot(columns):
        return jnp.where(iota_type == columns[:, 3:4], 1.0, 0.0).astype(BF16)

    def first_keys(blocks):
        for kb in blocks:
            kv[0, kb] = jnp.dot(
                onehot(jnp.transpose(packs[kb])), qkv_table[:, width:], preferred_element_type=F32
            ).astype(BF16)

    def first_rows(cols, r):
        which = onehot(cols)
        hs[r] = jnp.dot(which, table[0], preferred_element_type=F32).astype(BF16)
        heads_apart(jnp.dot(which, qkv_table[:, 0:width], preferred_element_type=F32), r)

    to_tanh = 0.5 / math.sqrt(head_dim)

    def unit(layer, r, blocks, first):
        last = layer == n_section - 1
        k = jnp.concatenate([kv[layer % 2, kb, :, 0:width] for kb in blocks], axis=0)
        s = lax.dot_general(qm[r], k, NT, preferred_element_type=F32)
        half = jnp.concatenate([half_pair[r, kb] for kb in blocks], axis=1)
        total = None
        gated = []
        for h in range(heads):
            t = jnp.tanh(s[h * blk : (h + 1) * blk, :] * to_tanh)
            term = gcs[layer, 1:2, h : h + 1] * t
            total = term if total is None else total + term
            if not last:
                gated.append((half * t + half).astype(BF16))
        for n, kb in enumerate(blocks):
            piece = total[:, n * blk : (n + 1) * blk]
            if layer == 0:
                coef_sum[r, kb] = piece
            else:
                coef_sum[r, kb] += piece
        if not last:
            v = jnp.concatenate([kv[layer % 2, kb, :, width:] for kb in blocks], axis=0)
            part = jnp.dot(jnp.concatenate(gated, axis=0), v, preferred_element_type=F32)
            if first:
                acc[r] = part
            else:
                acc[r] += part

    def finish(layer, r):
        message = acc[r, 0:blk, :]
        for h in range(1, heads):
            message = jnp.where(lane_head == h, acc[r, h * blk : (h + 1) * blk, :], message)
        message = (message * (1.0 / slots)).astype(BF16)
        h_new = (
            hs[r].astype(F32) + jnp.dot(message, outs[layer], preferred_element_type=F32)
        ).astype(BF16)
        hs[r] = h_new
        x = normed(h_new.astype(F32), gcs[layer + 1, 0:1, :])
        mine = 2 * y + sides[r]
        xs[layer, mine] = x
        part = xs.at[layer, mine]
        for n, to in reversed(list(enumerate(near))):
            send(part, part, x_ss.at[layer, r, n], x_rs.at[layer, mine], to)

    def prepare(layer):
        own = [xs[layer, 2 * y + sides[r]] for r in range(2)]
        for r in range(2):
            queries(own[r], layer + 1, r)
        keys(jnp.concatenate(own, axis=0), layer + 1, [2 * y + zh, 2 * y + other])

    def arrived(layer, r):
        blocks = [2 * y2 + sides[r] for y2 in ring]
        for kb in blocks:
            got(xs.at[layer - 1, kb], x_rs.at[layer - 1, kb])
        keys(jnp.concatenate([xs[layer - 1, kb] for kb in blocks], axis=0), layer, blocks)

    for y2 in ring:
        got(packs.at[2 * y2 + zh], pack_rs.at[2 * y2 + zh])
    cols_own = jnp.transpose(packs[at])
    pair_half(0, cols_own, near_blocks)
    first_keys(near_blocks)
    first_rows(cols_own, 0)
    unit(0, 0, near_blocks, True)
    got(code_got, code_rs)
    count(code_got, 1)
    for kb in far_blocks:
        got(packs.at[kb], pack_rs.at[kb])
    cols_far = jnp.transpose(packs[2 * y + other])
    own_cols = [cols_own, cols_far]
    pair_half(0, cols_own, far_blocks)
    first_keys(far_blocks)
    first_rows(cols_far, 1)
    unit(0, 0, far_blocks, False)
    weights_ready(1)
    finish(0, 0)
    pair_half(1, cols_far, near_blocks + far_blocks)
    unit(0, 1, near_blocks, True)
    unit(0, 1, far_blocks, False)
    finish(0, 1)
    prepare(0)

    def pull(r, blocks, parts):
        for kb in blocks:
            pj = packs[kb]
            w = half_pair[r, kb] * (coef_sum[r, kb] + coef_all)
            for d in range(3):
                parts[d] = parts[d] + w * (pj[d : d + 1, :] - own_cols[r][:, d : d + 1])
        return parts

    for layer in range(1, n_section):
        last = layer == n_section - 1
        for r in range(2):
            unit(layer, r, [2 * y + zh, 2 * y + other], True)
        arrived(layer, 0)
        for r in range(2):
            unit(layer, r, near_blocks[1:], False)
        if not last:
            weights_ready(layer + 1)
        else:
            coef_all = jnp.zeros((1, 1), F32)
            for b in range(n_section):
                coef_all = coef_all + jnp.sum(gcs[b, 1:2, :], axis=1, keepdims=True)
            for r in range(2):
                parts = pull(r, near_blocks + far_blocks[:1], [jnp.zeros((blk, blk), F32)] * 3)
                for d in range(3):
                    pulled[r, d] = parts[d]
        arrived(layer, 1)
        for r in range(2):
            unit(layer, r, far_blocks[1:], False)
            if not last:
                finish(layer, r)
        if not last:
            prepare(layer)

    column = lax.broadcasted_iota(jnp.int32, (blk, 8), 1)
    tile = jnp.zeros((blk, 8), F32)
    for r in range(2):
        parts = pull(r, far_blocks[1:], [pulled[r, d] for d in range(3)])
        for d in range(3):
            tile = jnp.where(column == 4 * r + d, jnp.sum(parts[d], axis=1, keepdims=True), tile)
    f_all[zh, me] = jnp.transpose(tile) * (1.0 / slots)
    before = list(sent)
    sent.clear()
    mine = f_all.at[zh, me]
    for n, m2 in enumerate(far_mates):
        to = {"member": m2, "atoms": 2 * y + other}
        send(mine, mine, f_ss.at[n_member + n], f_rs.at[zh, me], to)
    for n, m2 in enumerate(mates):
        send(mine, mine, f_ss.at[n], f_rs.at[zh, me], {"member": m2})

    for copy in before:
        copy.wait_send()
    row = lax.broadcasted_iota(jnp.int32, (8, blk), 0)

    def statistics(side):
        total = f_all[side, 0]
        for m in range(1, n_member):
            total = total + f_all[side, m]
        mean = total * (1.0 / n_member)
        square = jnp.zeros((8, blk), F32)
        for m in range(n_member):
            centered = f_all[side, m] - mean
            square = square + centered * centered
        dev = [
            jnp.sqrt(jnp.sum(square[4 * r : 4 * r + 4], axis=0, keepdims=True) * (1.0 / n_member))
            for r in range(2)
        ]
        return mean, dev

    for m2 in mates:
        got(f_all.at[zh, m2], f_rs.at[zh, m2])
    mean, dev = statistics(zh)
    for m2 in far_mates:
        got(f_all.at[other, m2], f_rs.at[other, m2])
    mean_far, dev_far = statistics(other)
    mean_far = mean_far[4:8]
    d_all[y] = jnp.where(
        row == 0,
        jnp.maximum(dev[0], dev[1]),
        jnp.where(row == 1, jnp.maximum(dev_far[0], dev_far[1]), 0.0),
    )
    for n, to in enumerate(near):
        send(d_all.at[y], d_all.at[y], d_ss.at[n], d_rs.at[y], to)
    for copy in sent[: -len(near)]:
        copy.wait_send()
    del sent[: -len(near)]
    first = zh == 0
    dev_out[0:1, :] = jnp.where(first, dev[0], dev_far[1])
    dev_out[1:2, :] = jnp.where(first, dev_far[1], dev[0])
    for d in range(3):
        here, there = mean[d : d + 1, :], mean_far[d : d + 1, :]
        mean_out[d, 0:1, :] = jnp.where(first, here, there)
        mean_out[d, 1:2, :] = jnp.where(first, there, here)
    for y2 in ring:
        got(d_all.at[y2], d_rs.at[y2])
    best = d_all[0]
    for y2 in range(1, n_y):
        best = jnp.maximum(best, d_all[y2])
    max_out[zh] = jnp.max(best[0:1, :])
    max_out[other] = jnp.max(best[1:2, :])

    all_left()


def hand_on(dev_in, max_in, mean_in, dev_out, max_out, mean_out, sem):
    copies = [
        pltpu.make_async_copy(a, b, sem.at[n])
        for n, (a, b) in enumerate([(dev_in, dev_out), (max_in, max_out), (mean_in, mean_out)])
    ]
    for c in copies:
        c.start()
    for c in copies:
        c.wait()


def shards(
    positions,
    atom_types,
    neighbors,
    nbr_mask,
    type_table,
    norm_gain,
    proj_weight,
    out_weight,
    force_coef,
):
    n_section = lax.axis_size("section")
    n_member = lax.axis_size("member")
    n_atoms = lax.axis_size("atoms")
    n_y = n_atoms // 2
    heads = force_coef.shape[2]
    width = type_table.shape[2]
    blk = atom_types.shape[1]
    slots = neighbors.shape[2]
    frames = atom_types.shape[0]
    dims = (n_member, n_section, n_y, heads, width // heads, slots)
    dma = pltpu.SemaphoreType.DMA
    vmem = pltpu.VMEM
    scratch = [
        vmem((3, frames, blk), F32),
        vmem((frames, blk), jnp.int32),
        vmem((2, blk, slots), jnp.int32),
        vmem((2, blk, slots), jnp.int32),
        vmem(type_table.shape, BF16),
        vmem(norm_gain.shape, BF16),
        vmem(force_coef.shape, BF16),
        vmem((2, 8, blk), F32),
        vmem((n_atoms, 8, blk), F32),
        vmem((blk, slots), jnp.int32),
        vmem((blk, slots), jnp.int32),
        vmem((blk, slots), jnp.int32),
        vmem((8, width), F32),
        vmem((n_section, 8, width), F32),
        vmem((n_section, width, 3 * width), BF16),
        vmem((n_section, width, width), BF16),
        vmem((2 * blk * 8, blk), F32),
        vmem((2, n_atoms, blk, blk), F32),
        vmem((2, n_atoms, blk, blk), F32),
        vmem((n_section - 1, n_atoms, blk, width), BF16),
        vmem((2, n_atoms, blk, 2 * width), BF16),
        vmem((2, heads * blk, width), BF16),
        vmem((2, heads * blk, width), F32),
        vmem((2, blk, width), BF16),
        vmem((2, n_member, 8, blk), F32),
        vmem((n_y, 8, blk), F32),
        vmem((2, 3, blk, blk), F32),
        dma((9,)),
        dma((n_atoms,)),
        dma((n_atoms,)),
        dma,
        dma,
        dma((3, n_section)),
        dma((3, n_section)),
        dma((n_section - 1, 2, n_y)),
        dma((n_section - 1, n_atoms)),
        dma((2 * n_member,)),
        dma((2, n_member)),
        dma((n_y,)),
        dma((n_y,)),
    ]
    own_frames = frames // n_section
    results = (
        jax.ShapeDtypeStruct((own_frames, blk), F32),
        jax.ShapeDtypeStruct((own_frames,), F32),
        jax.ShapeDtypeStruct((3, own_frames, blk), F32),
    )
    made = pl.pallas_call(
        functools.partial(kernel, dims),
        out_shape=results,
        in_specs=[pl.BlockSpec(memory_space=pltpu.HBM)] * 9,
        out_specs=(
            pl.BlockSpec(memory_space=pltpu.VMEM),
            pl.BlockSpec(memory_space=pltpu.SMEM),
            pl.BlockSpec(memory_space=pltpu.VMEM),
        ),
        scratch_shapes=scratch,
        compiler_params=pltpu.CompilerParams(
            collective_id=0, has_side_effects=True, vmem_limit_bytes=56 * 1024 * 1024
        ),
        name="committee",
    )(
        jnp.transpose(positions, (1, 0, 2)),
        atom_types,
        neighbors,
        nbr_mask,
        type_table,
        norm_gain,
        proj_weight,
        out_weight,
        force_coef,
    )
    atom_dev, max_dev, mean_force = pl.pallas_call(
        hand_on,
        out_shape=results,
        in_specs=[pl.BlockSpec(memory_space=pl.ANY)] * 3,
        out_specs=(pl.BlockSpec(memory_space=pl.ANY),) * 3,
        scratch_shapes=[dma((3,))],
        name="outputs",
    )(*made)
    return (atom_dev, max_dev, jnp.transpose(mean_force, (1, 0, 2)))


def solution(mesh):
    return jax.shard_map(
        shards,
        mesh=mesh,
        in_specs=(
            P(None, None, "atoms"),
            P(None, "atoms"),
            P(None, "atoms", None),
            P(None, "atoms", None),
            P("member", None, None),
            P("member", "section", None),
            P("member", "section", None, None),
            P("member", "section", None, None),
            P("member", "section", None),
        ),
        out_specs=(P("section", "atoms"), P("section"), P("section", None, "atoms")),
        check_vma=False,
    )
```

```python
import functools
import math

import jax
import jax.numpy as jnp
from jax import lax
from jax.experimental import pallas as pl
from jax.experimental.pallas import tpu as pltpu
from jax.sharding import PartitionSpec as P

F32 = jnp.float32
BF16 = jnp.bfloat16
NT = (((1,), (1,)), ((), ()))


def kernel(
    dims,
    pos_hbm,
    types_hbm,
    nbr_hbm,
    mask_hbm,
    table_hbm,
    gain_hbm,
    proj_hbm,
    outw_hbm,
    coef_hbm,
    dev_out,
    max_out,
    mean_out,
    pos_in,
    types_in,
    nbr_in,
    mask_in,
    table,
    gain_in,
    coef_in,
    pack_src,
    packs,
    code_own,
    code_src,
    code_got,
    gc_src,
    gcs,
    projs,
    outs,
    counts,
    half_pair,
    coef_sum,
    xs,
    kv,
    qm,
    acc,
    hs,
    f_all,
    d_all,
    pulled,
    in_sem,
    pack_ss,
    pack_rs,
    code_ss,
    code_rs,
    w_ss,
    w_rs,
    x_ss,
    x_rs,
    f_ss,
    f_rs,
    d_ss,
    d_rs,
):
    n_member, n_section, n_y, heads, head_dim, slots = dims
    width = heads * head_dim
    n_atoms = 2 * n_y
    blk = 128
    me = lax.axis_index("member")
    sec = lax.axis_index("section")
    at = lax.axis_index("atoms")
    y = at // 2
    zh = at % 2
    other = 1 - zh
    sides = (zh, other)
    mirror = (n_member // 2 - 1 - me // 2) * 2 + me % 2

    turns = list(dict.fromkeys(k for k in (1, n_y - 1, 2) if 0 < k < n_y))
    ring = [(y + k) % n_y for k in turns]
    near = [{"atoms": 2 * y2 + zh} for y2 in ring]
    across = [{"atoms": 2 * y2 + other, "member": mirror} for y2 in [y] + ring]
    sec_turns = list(dict.fromkeys((1, n_section - 1, 2)))
    sec_peers = [{"section": (sec + k) % n_section} for k in sec_turns]
    mates = [(me + k) % n_member for k in range(1, n_member)]

    barrier = pltpu.get_barrier_semaphore()
    far_mates = [(me + k) % n_member for k in range(n_member)]
    partners = across[1:] + [{"member": m2, "atoms": 2 * y + other} for m2 in far_mates]
    partners = partners + near + sec_peers + [{"member": m2} for m2 in mates]
    n_far = n_y - 1 + n_member

    def greet(devices):
        for device in devices:
            pl.semaphore_signal(
                barrier, inc=1, device_id=device, device_id_type=pl.DeviceIdType.MESH
            )

    greet(partners[:n_far])

    frames2 = pl.ds(2 * sec, 2)
    loads = [
        pltpu.make_async_copy(pos_hbm, pos_in, in_sem.at[0]),
        pltpu.make_async_copy(types_hbm, types_in, in_sem.at[1]),
        pltpu.make_async_copy(nbr_hbm.at[frames2], nbr_in, in_sem.at[2]),
        pltpu.make_async_copy(mask_hbm.at[frames2], mask_in, in_sem.at[3]),
        pltpu.make_async_copy(gain_hbm, gain_in, in_sem.at[4]),
        pltpu.make_async_copy(coef_hbm, coef_in, in_sem.at[5]),
        pltpu.make_async_copy(proj_hbm.at[0, 0], projs.at[sec], in_sem.at[6]),
        pltpu.make_async_copy(outw_hbm.at[0, 0], outs.at[sec], in_sem.at[7]),
        pltpu.make_async_copy(table_hbm, table, in_sem.at[8]),
    ]
    for c in loads:
        c.start()
    greet(partners[n_far:])

    def remote(src, dst, ss, rs, device):
        return pltpu.make_async_remote_copy(
            src_ref=src,
            dst_ref=dst,
            send_sem=ss,
            recv_sem=rs,
            device_id=device,
            device_id_type=pl.DeviceIdType.MESH,
        )

    sent = []

    def send(*what):
        copy = remote(*what)
        copy.start()
        sent.append(copy)

    def all_left():
        while sent:
            sent.pop(0).wait_send()

    def got(dst, rs):
        remote(dst, dst, x_ss.at[0, 0, 0], rs, sec_peers[0]).wait_recv()

    loads[0].wait()
    loads[1].wait()
    pack_src[...] = jnp.zeros_like(pack_src)
    for r in range(2):
        frame = pl.ds(2 * sec + sides[r], 1)
        for d in range(3):
            pack_src[r, d : d + 1, :] = pos_in[d, frame, :]
        pack_src[r, 3:4, :] = types_in[frame, :].astype(F32)
    packs[at] = pack_src[0]
    pl.semaphore_wait(barrier, len(partners))
    for n, to in enumerate(across):
        send(pack_src.at[1], packs.at[at], pack_ss.at[n], pack_rs.at[at], to)

    for c in loads[4:8]:
        c.wait()
    gc_src[...] = jnp.zeros_like(gc_src)
    gc_src[0:1, :] = gain_in[0].astype(F32)
    gc_src[1:2, 0:heads] = coef_in[0].astype(F32)
    gcs[sec] = gc_src[...]
    shares = []
    for a, b, what in (
        (projs.at[sec], projs.at[sec], 1),
        (gc_src, gcs.at[sec], 0),
        (outs.at[sec], outs.at[sec], 2),
    ):
        for n, to in enumerate(sec_peers):
            shares.append(remote(a, b, w_ss.at[what, n], w_rs.at[what, sec], to))
    sent.extend(shares)

    def share(when):
        @pl.when(when)
        def _():
            for copy in shares:
                copy.start()

    share(sec == 0)

    loads[2].wait()
    loads[3].wait()
    unused = n_atoms * blk
    code_src[...] = nbr_in[other] + jnp.where(mask_in[other] != 0, 0, unused)
    send(code_src, code_got, code_ss, code_rs, across[0])
    for n, to in enumerate(near):
        send(pack_src.at[0], packs.at[at], pack_ss.at[n_y + n], pack_rs.at[at], to)
    code_own[...] = nbr_in[zh] + jnp.where(mask_in[zh] != 0, 0, unused)

    iota_hi = lax.broadcasted_iota(jnp.int32, (8, blk), 0)
    iota_lo = lax.broadcasted_iota(jnp.int32, (blk, blk), 0)
    none = jnp.zeros((8, blk), F32)

    def count(code_ref, r):
        code = code_ref[...]
        hi = lax.shift_right_logical(code, 7)
        lo = jnp.bitwise_and(code, blk - 1)
        for i in range(0, blk, 2):
            left = [
                jnp.where(iota_hi == hi[i + e : i + e + 1, :], 1.0, 0.0).astype(F32)
                for e in (0, 1)
            ]
            lhs = jnp.concatenate(
                [
                    jnp.concatenate([left[0], none], axis=1),
                    jnp.concatenate([none, left[1]], axis=1),
                ],
                axis=0,
            ).astype(BF16)
            rhs = jnp.concatenate(
                [
                    jnp.where(iota_lo == lo[i + e : i + e + 1, :], 1.0, 0.0).astype(BF16)
                    for e in (0, 1)
                ],
                axis=1,
            )
            both = lax.dot_general(lhs, rhs, NT, preferred_element_type=F32)
            first_row = (r * blk + i) * 8
            counts[first_row : first_row + 16, :] = both

    count(code_own, 0)
    share(sec != 0)

    near_blocks = [2 * y2 + zh for y2 in [y] + ring]
    far_blocks = [2 * y2 + other for y2 in [y] + ring]

    def pair_half(r, cols, blocks):
        for kb in blocks:
            pj = packs[kb]
            dist = jnp.zeros((blk, blk), F32)
            for d in range(3):
                delta = pj[d : d + 1, :] - cols[:, d : d + 1]
                dist = dist + delta * delta
            cnt = counts[pl.ds(r * blk * 8 + kb, blk, stride=8), :]
            half_pair[r, kb] = 0.5 * cnt / (1.0 + 0.125 * dist)

    def normed(hf, gain):
        return (hf * lax.rsqrt(jnp.mean(hf * hf, -1, keepdims=True) + 1e-06) * gain).astype(BF16)

    lane_head = lax.broadcasted_iota(jnp.int32, (blk, width), 1) // head_dim

    def heads_apart(q, r):
        for h in range(heads):
            qm[r, h * blk : (h + 1) * blk, :] = jnp.where(lane_head == h, q, 0.0).astype(BF16)

    def queries(x, layer, r):
        heads_apart(jnp.dot(x, projs[layer, :, 0:width], preferred_element_type=F32), r)

    def keys(x, layer, blocks):
        n_kv = width if layer == n_section - 1 else 2 * width
        out = jnp.dot(
            x, projs[layer, :, width : width + n_kv], preferred_element_type=F32
        ).astype(BF16)
        for n, kb in enumerate(blocks):
            kv[layer % 2, kb, :, 0:n_kv] = out[n * blk : (n + 1) * blk]

    def weights_ready(layer):
        @pl.when(sec != layer)
        def _():
            got(gcs.at[layer], w_rs.at[0, layer])
            got(projs.at[layer], w_rs.at[1, layer])
            got(outs.at[layer], w_rs.at[2, layer])

    loads[8].wait()
    weights_ready(0)

    x_table = normed(table[0].astype(F32), gcs[0, 0:1, :])
    qkv_table = jnp.dot(x_table, projs[0], preferred_element_type=F32).astype(BF16)
    iota_type = lax.broadcasted_iota(jnp.int32, (blk, blk), 1).astype(F32)

    def onehot(columns):
        return jnp.where(iota_type == columns[:, 3:4], 1.0, 0.0).astype(BF16)

    def first_keys(blocks):
        for kb in blocks:
            kv[0, kb] = jnp.dot(
                onehot(jnp.transpose(packs[kb])), qkv_table[:, width:], preferred_element_type=F32
            ).astype(BF16)

    def first_rows(cols, r):
        which = onehot(cols)
        hs[r] = jnp.dot(which, table[0], preferred_element_type=F32).astype(BF16)
        heads_apart(jnp.dot(which, qkv_table[:, 0:width], preferred_element_type=F32), r)

    to_tanh = 0.5 / math.sqrt(head_dim)

    def unit(layer, r, blocks, first):
        last = layer == n_section - 1
        k = jnp.concatenate([kv[layer % 2, kb, :, 0:width] for kb in blocks], axis=0)
        s = lax.dot_general(qm[r], k, NT, preferred_element_type=F32)
        half = jnp.concatenate([half_pair[r, kb] for kb in blocks], axis=1)
        total = None
        gated = []
        for h in range(heads):
            t = jnp.tanh(s[h * blk : (h + 1) * blk, :] * to_tanh)
            term = gcs[layer, 1:2, h : h + 1] * t
            total = term if total is None else total + term
            if not last:
                gated.append((half * t + half).astype(BF16))
        for n, kb in enumerate(blocks):
            piece = total[:, n * blk : (n + 1) * blk]
            if layer == 0:
                coef_sum[r, kb] = piece
            else:
                coef_sum[r, kb] += piece
        if not last:
            v = jnp.concatenate([kv[layer % 2, kb, :, width:] for kb in blocks], axis=0)
            part = jnp.dot(jnp.concatenate(gated, axis=0), v, preferred_element_type=F32)
            if first:
                acc[r] = part
            else:
                acc[r] += part

    def finish(layer, r):
        message = acc[r, 0:blk, :]
        for h in range(1, heads):
            message = jnp.where(lane_head == h, acc[r, h * blk : (h + 1) * blk, :], message)
        message = (message * (1.0 / slots)).astype(BF16)
        h_new = (
            hs[r].astype(F32) + jnp.dot(message, outs[layer], preferred_element_type=F32)
        ).astype(BF16)
        hs[r] = h_new
        x = normed(h_new.astype(F32), gcs[layer + 1, 0:1, :])
        mine = 2 * y + sides[r]
        xs[layer, mine] = x
        part = xs.at[layer, mine]
        for n, to in reversed(list(enumerate(near))):
            send(part, part, x_ss.at[layer, r, n], x_rs.at[layer, mine], to)

    def prepare(layer):
        own = [xs[layer, 2 * y + sides[r]] for r in range(2)]
        for r in range(2):
            queries(own[r], layer + 1, r)
        keys(jnp.concatenate(own, axis=0), layer + 1, [2 * y + zh, 2 * y + other])

    def arrived(layer, r):
        blocks = [2 * y2 + sides[r] for y2 in ring]
        for kb in blocks:
            got(xs.at[layer - 1, kb], x_rs.at[layer - 1, kb])
        keys(jnp.concatenate([xs[layer - 1, kb] for kb in blocks], axis=0), layer, blocks)

    for y2 in ring:
        got(packs.at[2 * y2 + zh], pack_rs.at[2 * y2 + zh])
    cols_own = jnp.transpose(packs[at])
    pair_half(0, cols_own, near_blocks)
    first_keys(near_blocks)
    first_rows(cols_own, 0)
    unit(0, 0, near_blocks, True)
    got(code_got, code_rs)
    count(code_got, 1)
    for kb in far_blocks:
        got(packs.at[kb], pack_rs.at[kb])
    cols_far = jnp.transpose(packs[2 * y + other])
    own_cols = [cols_own, cols_far]
    pair_half(0, cols_own, far_blocks)
    first_keys(far_blocks)
    first_rows(cols_far, 1)
    unit(0, 0, far_blocks, False)
    weights_ready(1)
    finish(0, 0)
    pair_half(1, cols_far, near_blocks + far_blocks)
    unit(0, 1, near_blocks, True)
    unit(0, 1, far_blocks, False)
    finish(0, 1)
    prepare(0)

    def pull(r, blocks, parts):
        for kb in blocks:
            pj = packs[kb]
            w = half_pair[r, kb] * (coef_sum[r, kb] + coef_all)
            for d in range(3):
                parts[d] = parts[d] + w * (pj[d : d + 1, :] - own_cols[r][:, d : d + 1])
        return parts

    for layer in range(1, n_section):
        last = layer == n_section - 1
        for r in range(2):
            unit(layer, r, [2 * y + zh, 2 * y + other], True)
        arrived(layer, 0)
        for r in range(2):
            unit(layer, r, near_blocks[1:], False)
        if not last:
            weights_ready(layer + 1)
        else:
            coef_all = jnp.zeros((1, 1), F32)
            for b in range(n_section):
                coef_all = coef_all + jnp.sum(gcs[b, 1:2, :], axis=1, keepdims=True)
            for r in range(2):
                parts = pull(r, near_blocks + far_blocks[:1], [jnp.zeros((blk, blk), F32)] * 3)
                for d in range(3):
                    pulled[r, d] = parts[d]
        arrived(layer, 1)
        for r in range(2):
            unit(layer, r, far_blocks[1:], False)
            if not last:
                finish(layer, r)
        if not last:
            prepare(layer)

    column = lax.broadcasted_iota(jnp.int32, (blk, 8), 1)
    tile = jnp.zeros((blk, 8), F32)
    for r in range(2):
        parts = pull(r, far_blocks[1:], [pulled[r, d] for d in range(3)])
        for d in range(3):
            tile = jnp.where(column == 4 * r + d, jnp.sum(parts[d], axis=1, keepdims=True), tile)
    f_all[zh, me] = jnp.transpose(tile) * (1.0 / slots)
    before = list(sent)
    sent.clear()
    mine = f_all.at[zh, me]
    for n, m2 in enumerate(far_mates):
        to = {"member": m2, "atoms": 2 * y + other}
        send(mine, mine, f_ss.at[n_member + n], f_rs.at[zh, me], to)
    for n, m2 in enumerate(mates):
        send(mine, mine, f_ss.at[n], f_rs.at[zh, me], {"member": m2})

    for copy in before:
        copy.wait_send()
    row = lax.broadcasted_iota(jnp.int32, (8, blk), 0)

    def statistics(side):
        total = f_all[side, 0]
        for m in range(1, n_member):
            total = total + f_all[side, m]
        mean = total * (1.0 / n_member)
        square = jnp.zeros((8, blk), F32)
        for m in range(n_member):
            centered = f_all[side, m] - mean
            square = square + centered * centered
        dev = [
            jnp.sqrt(jnp.sum(square[4 * r : 4 * r + 4], axis=0, keepdims=True) * (1.0 / n_member))
            for r in range(2)
        ]
        return mean, dev

    for m2 in mates:
        got(f_all.at[zh, m2], f_rs.at[zh, m2])
    mean, dev = statistics(zh)
    for m2 in far_mates:
        got(f_all.at[other, m2], f_rs.at[other, m2])
    mean_far, dev_far = statistics(other)
    mean_far = mean_far[4:8]
    d_all[y] = jnp.where(
        row == 0,
        jnp.maximum(dev[0], dev[1]),
        jnp.where(row == 1, jnp.maximum(dev_far[0], dev_far[1]), 0.0),
    )
    for n, to in enumerate(near):
        send(d_all.at[y], d_all.at[y], d_ss.at[n], d_rs.at[y], to)
    for copy in sent[: -len(near)]:
        copy.wait_send()
    del sent[: -len(near)]
    first = zh == 0
    dev_out[0:1, :] = jnp.where(first, dev[0], dev_far[1])
    dev_out[1:2, :] = jnp.where(first, dev_far[1], dev[0])
    for d in range(3):
        here, there = mean[d : d + 1, :], mean_far[d : d + 1, :]
        mean_out[d, 0:1, :] = jnp.where(first, here, there)
        mean_out[d, 1:2, :] = jnp.where(first, there, here)
    for y2 in ring:
        got(d_all.at[y2], d_rs.at[y2])
    best = d_all[0]
    for y2 in range(1, n_y):
        best = jnp.maximum(best, d_all[y2])
    max_out[zh] = jnp.max(best[0:1, :])
    max_out[other] = jnp.max(best[1:2, :])

    all_left()


def hand_on(dev_in, max_in, mean_in, dev_out, max_out, mean_out, sem):
    copies = [
        pltpu.make_async_copy(a, b, sem.at[n])
        for n, (a, b) in enumerate([(dev_in, dev_out), (max_in, max_out), (mean_in, mean_out)])
    ]
    for c in copies:
        c.start()
    for c in copies:
        c.wait()


def shards(
    positions,
    atom_types,
    neighbors,
    nbr_mask,
    type_table,
    norm_gain,
    proj_weight,
    out_weight,
    force_coef,
):
    n_section = lax.axis_size("section")
    n_member = lax.axis_size("member")
    n_atoms = lax.axis_size("atoms")
    n_y = n_atoms // 2
    heads = force_coef.shape[2]
    width = type_table.shape[2]
    blk = atom_types.shape[1]
    slots = neighbors.shape[2]
    frames = atom_types.shape[0]
    dims = (n_member, n_section, n_y, heads, width // heads, slots)
    dma = pltpu.SemaphoreType.DMA
    vmem = pltpu.VMEM
    scratch = [
        vmem((3, frames, blk), F32),
        vmem((frames, blk), jnp.int32),
        vmem((2, blk, slots), jnp.int32),
        vmem((2, blk, slots), jnp.int32),
        vmem(type_table.shape, BF16),
        vmem(norm_gain.shape, BF16),
        vmem(force_coef.shape, BF16),
        vmem((2, 8, blk), F32),
        vmem((n_atoms, 8, blk), F32),
        vmem((blk, slots), jnp.int32),
        vmem((blk, slots), jnp.int32),
        vmem((blk, slots), jnp.int32),
        vmem((8, width), F32),
        vmem((n_section, 8, width), F32),
        vmem((n_section, width, 3 * width), BF16),
        vmem((n_section, width, width), BF16),
        vmem((2 * blk * 8, blk), F32),
        vmem((2, n_atoms, blk, blk), F32),
        vmem((2, n_atoms, blk, blk), F32),
        vmem((n_section - 1, n_atoms, blk, width), BF16),
        vmem((2, n_atoms, blk, 2 * width), BF16),
        vmem((2, heads * blk, width), BF16),
        vmem((2, heads * blk, width), F32),
        vmem((2, blk, width), BF16),
        vmem((2, n_member, 8, blk), F32),
        vmem((n_y, 8, blk), F32),
        vmem((2, 3, blk, blk), F32),
        dma((9,)),
        dma((n_atoms,)),
        dma((n_atoms,)),
        dma,
        dma,
        dma((3, n_section)),
        dma((3, n_section)),
        dma((n_section - 1, 2, n_y)),
        dma((n_section - 1, n_atoms)),
        dma((2 * n_member,)),
        dma((2, n_member)),
        dma((n_y,)),
        dma((n_y,)),
    ]
    own_frames = frames // n_section
    results = (
        jax.ShapeDtypeStruct((own_frames, blk), F32),
        jax.ShapeDtypeStruct((own_frames,), F32),
        jax.ShapeDtypeStruct((3, own_frames, blk), F32),
    )
    made = pl.pallas_call(
        functools.partial(kernel, dims),
        out_shape=results,
        in_specs=[pl.BlockSpec(memory_space=pltpu.HBM)] * 9,
        out_specs=(
            pl.BlockSpec(memory_space=pltpu.VMEM),
            pl.BlockSpec(memory_space=pltpu.SMEM),
            pl.BlockSpec(memory_space=pltpu.VMEM),
        ),
        scratch_shapes=scratch,
        compiler_params=pltpu.CompilerParams(
            collective_id=0, has_side_effects=True, vmem_limit_bytes=56 * 1024 * 1024
        ),
        name="committee",
    )(
        jnp.transpose(positions, (1, 0, 2)),
        atom_types,
        neighbors,
        nbr_mask,
        type_table,
        norm_gain,
        proj_weight,
        out_weight,
        force_coef,
    )
    atom_dev, max_dev, mean_force = pl.pallas_call(
        hand_on,
        out_shape=results,
        in_specs=[pl.BlockSpec(memory_space=pl.ANY)] * 3,
        out_specs=(pl.BlockSpec(memory_space=pl.ANY),) * 3,
        scratch_shapes=[dma((3,))],
        name="outputs",
    )(*made)
    return (atom_dev, max_dev, jnp.transpose(mean_force, (1, 0, 2)))


def solution(mesh):
    return jax.shard_map(
        shards,
        mesh=mesh,
        in_specs=(
            P(None, None, "atoms"),
            P(None, "atoms"),
            P(None, "atoms", None),
            P(None, "atoms", None),
            P("member", None, None),
            P("member", "section", None),
            P("member", "section", None, None),
            P("member", "section", None, None),
            P("member", "section", None),
        ),
        out_specs=(P("section", "atoms"), P("section"), P("section", None, "atoms")),
        check_vma=False,
    )
```

```python
import functools
import math

import jax
import jax.numpy as jnp
from jax import lax
from jax.experimental import pallas as pl
from jax.experimental.pallas import tpu as pltpu
from jax.sharding import PartitionSpec as P

F32 = jnp.float32
BF16 = jnp.bfloat16
NT = (((1,), (1,)), ((), ()))


def kernel(
    dims,
    pos_hbm,
    types_hbm,
    nbr_hbm,
    mask_hbm,
    table_hbm,
    gain_hbm,
    proj_hbm,
    outw_hbm,
    coef_hbm,
    dev_out,
    max_out,
    mean_out,
    pos_in,
    types_in,
    nbr_in,
    mask_in,
    table,
    gain_in,
    coef_in,
    pack_src,
    packs,
    code_own,
    code_src,
    code_got,
    gc_src,
    gcs,
    projs,
    outs,
    counts,
    half_pair,
    coef_sum,
    xs,
    kv,
    qm,
    acc,
    hs,
    f_all,
    d_all,
    pulled,
    in_sem,
    pack_ss,
    pack_rs,
    code_ss,
    code_rs,
    w_ss,
    w_rs,
    x_ss,
    x_rs,
    f_ss,
    f_rs,
    d_ss,
    d_rs,
):
    n_member, n_section, n_y, heads, head_dim, slots = dims
    width = heads * head_dim
    n_atoms = 2 * n_y
    blk = 128
    me = lax.axis_index("member")
    sec = lax.axis_index("section")
    at = lax.axis_index("atoms")
    y = at // 2
    zh = at % 2
    other = 1 - zh
    sides = (zh, other)
    mirror = (n_member // 2 - 1 - me // 2) * 2 + me % 2

    turns = list(dict.fromkeys(k for k in (1, n_y - 1, 2) if 0 < k < n_y))
    ring = [(y + k) % n_y for k in turns]
    near = [{"atoms": 2 * y2 + zh} for y2 in ring]
    across = [{"atoms": 2 * y2 + other, "member": mirror} for y2 in [y] + ring]
    sec_turns = list(dict.fromkeys((1, n_section - 1, 2)))
    sec_peers = [{"section": (sec + k) % n_section} for k in sec_turns]
    mates = [(me + k) % n_member for k in range(1, n_member)]

    barrier = pltpu.get_barrier_semaphore()
    far_mates = [(me + k) % n_member for k in range(n_member)]
    partners = across[1:] + [{"member": m2, "atoms": 2 * y + other} for m2 in far_mates]
    partners = partners + near + sec_peers + [{"member": m2} for m2 in mates]
    n_far = n_y - 1 + n_member

    def greet(devices):
        for device in devices:
            pl.semaphore_signal(
                barrier, inc=1, device_id=device, device_id_type=pl.DeviceIdType.MESH
            )

    greet(partners[:n_far])

    frames2 = pl.ds(2 * sec, 2)
    loads = [
        pltpu.make_async_copy(pos_hbm, pos_in, in_sem.at[0]),
        pltpu.make_async_copy(types_hbm, types_in, in_sem.at[1]),
        pltpu.make_async_copy(nbr_hbm.at[frames2], nbr_in, in_sem.at[2]),
        pltpu.make_async_copy(mask_hbm.at[frames2], mask_in, in_sem.at[3]),
        pltpu.make_async_copy(gain_hbm, gain_in, in_sem.at[4]),
        pltpu.make_async_copy(coef_hbm, coef_in, in_sem.at[5]),
        pltpu.make_async_copy(proj_hbm.at[0, 0], projs.at[sec], in_sem.at[6]),
        pltpu.make_async_copy(outw_hbm.at[0, 0], outs.at[sec], in_sem.at[7]),
        pltpu.make_async_copy(table_hbm, table, in_sem.at[8]),
    ]
    for c in loads:
        c.start()
    greet(partners[n_far:])

    def remote(src, dst, ss, rs, device):
        return pltpu.make_async_remote_copy(
            src_ref=src,
            dst_ref=dst,
            send_sem=ss,
            recv_sem=rs,
            device_id=device,
            device_id_type=pl.DeviceIdType.MESH,
        )

    sent = []

    def send(*what):
        copy = remote(*what)
        copy.start()
        sent.append(copy)

    def all_left():
        while sent:
            sent.pop(0).wait_send()

    def got(dst, rs):
        remote(dst, dst, x_ss.at[0, 0, 0], rs, sec_peers[0]).wait_recv()

    loads[0].wait()
    loads[1].wait()
    pack_src[...] = jnp.zeros_like(pack_src)
    for r in range(2):
        frame = pl.ds(2 * sec + sides[r], 1)
        for d in range(3):
            pack_src[r, d : d + 1, :] = pos_in[d, frame, :]
        pack_src[r, 3:4, :] = types_in[frame, :].astype(F32)
    packs[at] = pack_src[0]
    pl.semaphore_wait(barrier, len(partners))
    for n, to in enumerate(across):
        send(pack_src.at[1], packs.at[at], pack_ss.at[n], pack_rs.at[at], to)

    for c in loads[4:8]:
        c.wait()
    gc_src[...] = jnp.zeros_like(gc_src)
    gc_src[0:1, :] = gain_in[0].astype(F32)
    gc_src[1:2, 0:heads] = coef_in[0].astype(F32)
    gcs[sec] = gc_src[...]
    shares = []
    for a, b, what in (
        (gc_src, gcs.at[sec], 0),
        (projs.at[sec], projs.at[sec], 1),
        (outs.at[sec], outs.at[sec], 2),
    ):
        for n, to in enumerate(sec_peers):
            shares.append(remote(a, b, w_ss.at[what, n], w_rs.at[what, sec], to))
    sent.extend(shares)

    def share(when):
        @pl.when(when)
        def _():
            for copy in shares:
                copy.start()

    share(sec == 0)

    loads[2].wait()
    loads[3].wait()
    unused = n_atoms * blk
    code_src[...] = nbr_in[other] + jnp.where(mask_in[other] != 0, 0, unused)
    send(code_src, code_got, code_ss, code_rs, across[0])
    for n, to in enumerate(near):
        send(pack_src.at[0], packs.at[at], pack_ss.at[n_y + n], pack_rs.at[at], to)
    code_own[...] = nbr_in[zh] + jnp.where(mask_in[zh] != 0, 0, unused)

    iota_hi = lax.broadcasted_iota(jnp.int32, (8, blk), 0)
    iota_lo = lax.broadcasted_iota(jnp.int32, (blk, blk), 0)
    none = jnp.zeros((8, blk), F32)

    def count(code_ref, r):
        code = code_ref[...]
        hi = lax.shift_right_logical(code, 7)
        lo = jnp.bitwise_and(code, blk - 1)
        for i in range(0, blk, 2):
            left = [
                jnp.where(iota_hi == hi[i + e : i + e + 1, :], 1.0, 0.0).astype(F32)
                for e in (0, 1)
            ]
            lhs = jnp.concatenate(
                [
                    jnp.concatenate([left[0], none], axis=1),
                    jnp.concatenate([none, left[1]], axis=1),
                ],
                axis=0,
            ).astype(BF16)
            rhs = jnp.concatenate(
                [
                    jnp.where(iota_lo == lo[i + e : i + e + 1, :], 1.0, 0.0).astype(BF16)
                    for e in (0, 1)
                ],
                axis=1,
            )
            both = lax.dot_general(lhs, rhs, NT, preferred_element_type=F32)
            first_row = (r * blk + i) * 8
            counts[first_row : first_row + 16, :] = both

    count(code_own, 0)
    share(sec != 0)

    near_blocks = [2 * y2 + zh for y2 in [y] + ring]
    far_blocks = [2 * y2 + other for y2 in [y] + ring]

    def pair_half(r, cols, blocks):
        for kb in blocks:
            pj = packs[kb]
            dist = jnp.zeros((blk, blk), F32)
            for d in range(3):
                delta = pj[d : d + 1, :] - cols[:, d : d + 1]
                dist = dist + delta * delta
            cnt = counts[pl.ds(r * blk * 8 + kb, blk, stride=8), :]
            half_pair[r, kb] = 0.5 * cnt / (1.0 + 0.125 * dist)

    def normed(hf, gain):
        return (hf * lax.rsqrt(jnp.mean(hf * hf, -1, keepdims=True) + 1e-06) * gain).astype(BF16)

    lane_head = lax.broadcasted_iota(jnp.int32, (blk, width), 1) // head_dim

    def heads_apart(q, r):
        for h in range(heads):
            qm[r, h * blk : (h + 1) * blk, :] = jnp.where(lane_head == h, q, 0.0).astype(BF16)

    def queries(x, layer, r):
        heads_apart(jnp.dot(x, projs[layer, :, 0:width], preferred_element_type=F32), r)

    def keys(x, layer, blocks):
        n_kv = width if layer == n_section - 1 else 2 * width
        out = jnp.dot(
            x, projs[layer, :, width : width + n_kv], preferred_element_type=F32
        ).astype(BF16)
        for n, kb in enumerate(blocks):
            kv[layer % 2, kb, :, 0:n_kv] = out[n * blk : (n + 1) * blk]

    def gain_ready(layer):
        @pl.when(sec != layer)
        def _():
            got(gcs.at[layer], w_rs.at[0, layer])

    def proj_ready(layer):
        @pl.when(sec != layer)
        def _():
            got(projs.at[layer], w_rs.at[1, layer])

    def out_ready(layer):
        @pl.when(sec != layer)
        def _():
            got(outs.at[layer], w_rs.at[2, layer])

    loads[8].wait()
    gain_ready(0)
    proj_ready(0)

    x_table = normed(table[0].astype(F32), gcs[0, 0:1, :])
    qkv_table = jnp.dot(x_table, projs[0], preferred_element_type=F32).astype(BF16)
    iota_type = lax.broadcasted_iota(jnp.int32, (blk, blk), 1).astype(F32)

    def onehot(columns):
        return jnp.where(iota_type == columns[:, 3:4], 1.0, 0.0).astype(BF16)

    def first_keys(blocks):
        for kb in blocks:
            kv[0, kb] = jnp.dot(
                onehot(jnp.transpose(packs[kb])), qkv_table[:, width:], preferred_element_type=F32
            ).astype(BF16)

    def first_rows(cols, r):
        which = onehot(cols)
        hs[r] = jnp.dot(which, table[0], preferred_element_type=F32).astype(BF16)
        heads_apart(jnp.dot(which, qkv_table[:, 0:width], preferred_element_type=F32), r)

    to_tanh = 0.5 / math.sqrt(head_dim)

    def unit(layer, r, blocks, first):
        last = layer == n_section - 1
        k = jnp.concatenate([kv[layer % 2, kb, :, 0:width] for kb in blocks], axis=0)
        s = lax.dot_general(qm[r], k, NT, preferred_element_type=F32)
        half = jnp.concatenate([half_pair[r, kb] for kb in blocks], axis=1)
        total = None
        gated = []
        for h in range(heads):
            t = jnp.tanh(s[h * blk : (h + 1) * blk, :] * to_tanh)
            term = gcs[layer, 1:2, h : h + 1] * t
            total = term if total is None else total + term
            if not last:
                gated.append((half * t + half).astype(BF16))
        for n, kb in enumerate(blocks):
            piece = total[:, n * blk : (n + 1) * blk]
            if layer == 0:
                coef_sum[r, kb] = piece
            else:
                coef_sum[r, kb] += piece
        if not last:
            v = jnp.concatenate([kv[layer % 2, kb, :, width:] for kb in blocks], axis=0)
            part = jnp.dot(jnp.concatenate(gated, axis=0), v, preferred_element_type=F32)
            if first:
                acc[r] = part
            else:
                acc[r] += part

    def finish(layer, r):
        message = acc[r, 0:blk, :]
        for h in range(1, heads):
            message = jnp.where(lane_head == h, acc[r, h * blk : (h + 1) * blk, :], message)
        message = (message * (1.0 / slots)).astype(BF16)
        h_new = (
            hs[r].astype(F32) + jnp.dot(message, outs[layer], preferred_element_type=F32)
        ).astype(BF16)
        hs[r] = h_new
        x = normed(h_new.astype(F32), gcs[layer + 1, 0:1, :])
        mine = 2 * y + sides[r]
        xs[layer, mine] = x
        part = xs.at[layer, mine]
        for n, to in reversed(list(enumerate(near))):
            send(part, part, x_ss.at[layer, r, n], x_rs.at[layer, mine], to)

    def prepare(layer):
        proj_ready(layer + 1)
        own = [xs[layer, 2 * y + sides[r]] for r in range(2)]
        for r in range(2):
            queries(own[r], layer + 1, r)
        keys(jnp.concatenate(own, axis=0), layer + 1, [2 * y + zh, 2 * y + other])

    def arrived(layer, r):
        blocks = [2 * y2 + sides[r] for y2 in ring]
        for kb in blocks:
            got(xs.at[layer - 1, kb], x_rs.at[layer - 1, kb])
        keys(jnp.concatenate([xs[layer - 1, kb] for kb in blocks], axis=0), layer, blocks)

    for y2 in ring:
        got(packs.at[2 * y2 + zh], pack_rs.at[2 * y2 + zh])
    cols_own = jnp.transpose(packs[at])
    pair_half(0, cols_own, near_blocks)
    first_keys(near_blocks)
    first_rows(cols_own, 0)
    unit(0, 0, near_blocks, True)
    got(code_got, code_rs)
    count(code_got, 1)
    for kb in far_blocks:
        got(packs.at[kb], pack_rs.at[kb])
    cols_far = jnp.transpose(packs[2 * y + other])
    own_cols = [cols_own, cols_far]
    pair_half(0, cols_own, far_blocks)
    first_keys(far_blocks)
    first_rows(cols_far, 1)
    unit(0, 0, far_blocks, False)
    out_ready(0)
    gain_ready(1)
    finish(0, 0)
    pair_half(1, cols_far, near_blocks + far_blocks)
    unit(0, 1, near_blocks, True)
    unit(0, 1, far_blocks, False)
    finish(0, 1)
    prepare(0)

    def pull(r, blocks, parts):
        for kb in blocks:
            pj = packs[kb]
            w = half_pair[r, kb] * (coef_sum[r, kb] + coef_all)
            for d in range(3):
                parts[d] = parts[d] + w * (pj[d : d + 1, :] - own_cols[r][:, d : d + 1])
        return parts

    for layer in range(1, n_section):
        last = layer == n_section - 1
        for r in range(2):
            unit(layer, r, [2 * y + zh, 2 * y + other], True)
        arrived(layer, 0)
        for r in range(2):
            unit(layer, r, near_blocks[1:], False)
        if not last:
            out_ready(layer)
            gain_ready(layer + 1)
        else:
            coef_all = jnp.zeros((1, 1), F32)
            for b in range(n_section):
                coef_all = coef_all + jnp.sum(gcs[b, 1:2, :], axis=1, keepdims=True)
            for r in range(2):
                parts = pull(r, near_blocks + far_blocks[:1], [jnp.zeros((blk, blk), F32)] * 3)
                for d in range(3):
                    pulled[r, d] = parts[d]
        arrived(layer, 1)
        for r in range(2):
            unit(layer, r, far_blocks[1:], False)
            if not last:
                finish(layer, r)
        if not last:
            prepare(layer)

    out_ready(n_section - 1)
    column = lax.broadcasted_iota(jnp.int32, (blk, 8), 1)
    tile = jnp.zeros((blk, 8), F32)
    for r in range(2):
        parts = pull(r, far_blocks[1:], [pulled[r, d] for d in range(3)])
        for d in range(3):
            tile = jnp.where(column == 4 * r + d, jnp.sum(parts[d], axis=1, keepdims=True), tile)
    f_all[zh, me] = jnp.transpose(tile) * (1.0 / slots)
    before = list(sent)
    sent.clear()
    mine = f_all.at[zh, me]
    for n, m2 in enumerate(far_mates):
        to = {"member": m2, "atoms": 2 * y + other}
        send(mine, mine, f_ss.at[n_member + n], f_rs.at[zh, me], to)
    for n, m2 in enumerate(mates):
        send(mine, mine, f_ss.at[n], f_rs.at[zh, me], {"member": m2})

    for copy in before:
        copy.wait_send()
    row = lax.broadcasted_iota(jnp.int32, (8, blk), 0)

    def statistics(side):
        total = f_all[side, 0]
        for m in range(1, n_member):
            total = total + f_all[side, m]
        mean = total * (1.0 / n_member)
        square = jnp.zeros((8, blk), F32)
        for m in range(n_member):
            centered = f_all[side, m] - mean
            square = square + centered * centered
        dev = [
            jnp.sqrt(jnp.sum(square[4 * r : 4 * r + 4], axis=0, keepdims=True) * (1.0 / n_member))
            for r in range(2)
        ]
        return mean, dev

    for m2 in mates:
        got(f_all.at[zh, m2], f_rs.at[zh, m2])
    mean, dev = statistics(zh)
    for m2 in far_mates:
        got(f_all.at[other, m2], f_rs.at[other, m2])
    mean_far, dev_far = statistics(other)
    mean_far = mean_far[4:8]
    d_all[y] = jnp.where(
        row == 0,
        jnp.maximum(dev[0], dev[1]),
        jnp.where(row == 1, jnp.maximum(dev_far[0], dev_far[1]), 0.0),
    )
    for n, to in enumerate(near):
        send(d_all.at[y], d_all.at[y], d_ss.at[n], d_rs.at[y], to)
    for copy in sent[: -len(near)]:
        copy.wait_send()
    del sent[: -len(near)]
    first = zh == 0
    dev_out[0:1, :] = jnp.where(first, dev[0], dev_far[1])
    dev_out[1:2, :] = jnp.where(first, dev_far[1], dev[0])
    for d in range(3):
        here, there = mean[d : d + 1, :], mean_far[d : d + 1, :]
        mean_out[d, 0:1, :] = jnp.where(first, here, there)
        mean_out[d, 1:2, :] = jnp.where(first, there, here)
    for y2 in ring:
        got(d_all.at[y2], d_rs.at[y2])
    best = d_all[0]
    for y2 in range(1, n_y):
        best = jnp.maximum(best, d_all[y2])
    max_out[zh] = jnp.max(best[0:1, :])
    max_out[other] = jnp.max(best[1:2, :])

    all_left()


def hand_on(dev_in, max_in, mean_in, dev_out, max_out, mean_out, sem):
    copies = [
        pltpu.make_async_copy(a, b, sem.at[n])
        for n, (a, b) in enumerate([(dev_in, dev_out), (max_in, max_out), (mean_in, mean_out)])
    ]
    for c in copies:
        c.start()
    for c in copies:
        c.wait()


def shards(
    positions,
    atom_types,
    neighbors,
    nbr_mask,
    type_table,
    norm_gain,
    proj_weight,
    out_weight,
    force_coef,
):
    n_section = lax.axis_size("section")
    n_member = lax.axis_size("member")
    n_atoms = lax.axis_size("atoms")
    n_y = n_atoms // 2
    heads = force_coef.shape[2]
    width = type_table.shape[2]
    blk = atom_types.shape[1]
    slots = neighbors.shape[2]
    frames = atom_types.shape[0]
    dims = (n_member, n_section, n_y, heads, width // heads, slots)
    dma = pltpu.SemaphoreType.DMA
    vmem = pltpu.VMEM
    scratch = [
        vmem((3, frames, blk), F32),
        vmem((frames, blk), jnp.int32),
        vmem((2, blk, slots), jnp.int32),
        vmem((2, blk, slots), jnp.int32),
        vmem(type_table.shape, BF16),
        vmem(norm_gain.shape, BF16),
        vmem(force_coef.shape, BF16),
        vmem((2, 8, blk), F32),
        vmem((n_atoms, 8, blk), F32),
        vmem((blk, slots), jnp.int32),
        vmem((blk, slots), jnp.int32),
        vmem((blk, slots), jnp.int32),
        vmem((8, width), F32),
        vmem((n_section, 8, width), F32),
        vmem((n_section, width, 3 * width), BF16),
        vmem((n_section, width, width), BF16),
        vmem((2 * blk * 8, blk), F32),
        vmem((2, n_atoms, blk, blk), F32),
        vmem((2, n_atoms, blk, blk), F32),
        vmem((n_section - 1, n_atoms, blk, width), BF16),
        vmem((2, n_atoms, blk, 2 * width), BF16),
        vmem((2, heads * blk, width), BF16),
        vmem((2, heads * blk, width), F32),
        vmem((2, blk, width), BF16),
        vmem((2, n_member, 8, blk), F32),
        vmem((n_y, 8, blk), F32),
        vmem((2, 3, blk, blk), F32),
        dma((9,)),
        dma((n_atoms,)),
        dma((n_atoms,)),
        dma,
        dma,
        dma((3, n_section)),
        dma((3, n_section)),
        dma((n_section - 1, 2, n_y)),
        dma((n_section - 1, n_atoms)),
        dma((2 * n_member,)),
        dma((2, n_member)),
        dma((n_y,)),
        dma((n_y,)),
    ]
    own_frames = frames // n_section
    results = (
        jax.ShapeDtypeStruct((own_frames, blk), F32),
        jax.ShapeDtypeStruct((own_frames,), F32),
        jax.ShapeDtypeStruct((3, own_frames, blk), F32),
    )
    made = pl.pallas_call(
        functools.partial(kernel, dims),
        out_shape=results,
        in_specs=[pl.BlockSpec(memory_space=pltpu.HBM)] * 9,
        out_specs=(
            pl.BlockSpec(memory_space=pltpu.VMEM),
            pl.BlockSpec(memory_space=pltpu.SMEM),
            pl.BlockSpec(memory_space=pltpu.VMEM),
        ),
        scratch_shapes=scratch,
        compiler_params=pltpu.CompilerParams(
            collective_id=0, has_side_effects=True, vmem_limit_bytes=56 * 1024 * 1024
        ),
        name="committee",
    )(
        jnp.transpose(positions, (1, 0, 2)),
        atom_types,
        neighbors,
        nbr_mask,
        type_table,
        norm_gain,
        proj_weight,
        out_weight,
        force_coef,
    )
    atom_dev, max_dev, mean_force = pl.pallas_call(
        hand_on,
        out_shape=results,
        in_specs=[pl.BlockSpec(memory_space=pl.ANY)] * 3,
        out_specs=(pl.BlockSpec(memory_space=pl.ANY),) * 3,
        scratch_shapes=[dma((3,))],
        name="outputs",
    )(*made)
    return (atom_dev, max_dev, jnp.transpose(mean_force, (1, 0, 2)))


def solution(mesh):
    return jax.shard_map(
        shards,
        mesh=mesh,
        in_specs=(
            P(None, None, "atoms"),
            P(None, "atoms"),
            P(None, "atoms", None),
            P(None, "atoms", None),
            P("member", None, None),
            P("member", "section", None),
            P("member", "section", None, None),
            P("member", "section", None, None),
            P("member", "section", None),
        ),
        out_specs=(P("section", "atoms"), P("section"), P("section", None, "atoms")),
        check_vma=False,
    )
```
